32 devices in a mesh: seq: 4 (over y, x), user: 8 (over z, core).
Axes of the slice: x: 2, y: 2, z: 4, core: 2. Of those that a mesh axis runs over, the one named last changes fastest.
Arguments:
- events: bfloat16 [8, 512, 1536], P('user', 'seq'), may hold values from -6 to 6
- scenario: int32 [8, 512], P('user', 'seq'), may hold values from 0 to 7, as said below
- lengths: int32 [8, 4], P('user'), may hold values from 1 to 256, 512 in all within a row
- offsets: int32 [8, 4], P('user'), may hold values from 0 to 4, as said below
- gain: float32 [1536], replicated, may hold values from 0.1 to 1.9
- w_proj: bfloat16 [8, 1536, 3072], P('user'), may hold values from -0.15625 to 0.15625
- cotangent: bfloat16 [8, 512, 768], P('user', 'seq'), may hold values from -6 to 6
Outputs:
- output: bfloat16 [8, 512, 768], P('user', 'seq')
- grad_events: bfloat16 [8, 512, 1536], P('user', 'seq')
The draws below stay inside these ranges and needn't reach their ends.
Inputs may be any that keep to these rules, and one draw needn't show every extreme that they name: Among the 128 positions of one device (aligned blocks along a pack), no scenario is named more than 20 times; on every device one scenario is named exactly 20 times, the same one on all devices of one index of seq; the others share the remaining positions as evenly as possible. `offsets`: every pack has a history with 4.
All inputs are finite; a program needn't handle non-finite values.
Results may differ from the reference program's by a relative error of at most 0.009.
Values may be sent and summed in bfloat16 or wider, within the bound.
No kernel may reach another device: no remote copies, remote signals or barrier semaphores. Data moves between devices by JAX's collectives and lax.ppermute only.
A program may use at most 64 MiB of HBM per device.

```python
import math
import jax
import jax.numpy as jnp
import numpy as np
from jax import lax

D = 1536
HEADS = 6
HD = 128
SCEN = 8
WIN = 4
MB = 128
HIST = 4
ROWS = 128
INNER = 768
PROJ = 3072
SLICES = 1
SLICE = 3072
OWNERS = 8
PACK = 512
PACKS = 8
CAP = 20


def draw_scenario(key, part):
    block_count = PACKS * PACK // ROWS
    group_count = PACK // ROWS
    hot_seq = jax.random.randint(jax.random.fold_in(key, 11), (group_count,), 0, SCEN)
    hot_block = jnp.tile(hot_seq, block_count // group_count).astype(jnp.int32)
    block_keys = jax.random.split(jax.random.fold_in(key, 12), block_count)
    repeats = (ROWS - CAP) // (SCEN - 1) + 1

    def one_block(block_key, hot_id):
        first_key, second_key = jax.random.split(block_key)
        others = (hot_id + 1 + jax.random.permutation(first_key, SCEN - 1).astype(jnp.int32)) % SCEN
        filler = jnp.tile(others, repeats)[:ROWS - CAP]
        listed = jnp.concatenate([jnp.full((CAP,), hot_id, jnp.int32), filler.astype(jnp.int32)])
        return jax.random.permutation(second_key, listed)
    table = jax.vmap(one_block)(block_keys, hot_block)
    return table.reshape(PACKS, PACK).astype(jnp.int32)


def draw_offsets(key, part):
    base = jax.random.randint(jax.random.fold_in(key, 21), (PACKS, HIST), 0, WIN + 1)
    picked = jax.random.randint(jax.random.fold_in(key, 22), (PACKS, 1), 0, HIST)
    column = jnp.arange(HIST, dtype=jnp.int32)[None, :]
    return jnp.where(column == picked, WIN, base).astype(jnp.int32)


def block_levels(stream_key, dims, shards, least, largest):
    level, own = 1.0, jax.random.fold_in(stream_key, 6)
    for position, shards_of in shards:
        steps = jnp.exp(jax.random.uniform(jax.random.fold_in(own, position), (shards_of,), jnp.float32, least / len(shards), largest / len(shards)))
        level = level * jnp.repeat(steps, dims[position] // shards_of).reshape([-1 if axis == position else 1 for axis in range(len(dims))])
    return level


def length_profile(number_of, total, limit, slope):
    weights = [(1 << 20) // math.isqrt(grade ** slope) + 1 for grade in range(2, number_of + 1)]
    rest, given = total - limit - (number_of - 1), [1] * (number_of - 1)
    while rest > 0:
        candidates = [i for i in range(number_of - 1) if given[i] < limit]
        pool, budget = sum([weights[i] for i in candidates]), rest
        for i in candidates:
            extra = min(limit - given[i], max(1, budget * weights[i] // pool), rest)
            given[i] = given[i] + extra
            rest = rest - extra
    return np.array([limit] + given)


def uneven(stream_key, amount, total, reach, skew):
    if amount == 2:
        one = jax.random.randint(stream_key, (), max(1, total - reach), min(reach, total - 1) + 1)
        return jnp.stack([one, total - one])
    sizes = jnp.asarray(length_profile(amount, total, reach, skew), jnp.int32)
    couples = (amount - 1) // 2
    giver, taker = sizes[1:1 + 2 * couples:2], sizes[2:2 + 2 * couples:2]
    margin = jnp.minimum(giver - 1, reach - taker)
    shifted = jax.random.randint(jax.random.fold_in(stream_key, 1), (couples,), 0, 1 << 20) % (margin + 1)
    sizes = sizes.at[1:1 + 2 * couples:2].set(giver - shifted).at[2:2 + 2 * couples:2].set(taker + shifted)
    return sizes[jax.random.permutation(jax.random.fold_in(stream_key, 2), amount)]


def noise(rng, extent, deviation, bound, shards=(), kind=jnp.bfloat16):
    array = deviation * jax.random.normal(rng, extent, jnp.float32)
    if shards:
        array = array * block_levels(rng, extent, shards, -0.22, 0.18)
    return jnp.clip(array, -bound, bound).astype(kind)


def setup_inputs(seed: int = 0) -> dict:
    seeds = jax.random.split(jax.random.key(seed), 8)
    return {
        "events": noise(seeds[0], (PACKS, PACK, D), 1.0, 6.0, ((0, 8), (1, 4))),
        "scenario": draw_scenario(jax.random.fold_in(seeds[7], 71), 0),
        "lengths": jax.vmap(lambda own: uneven(own, HIST, PACK, PACK // 2, 2))(jax.random.split(seeds[2], PACKS)).reshape((PACKS, HIST)).astype(jnp.int32),
        "offsets": draw_offsets(jax.random.fold_in(seeds[7], 71), 0),
        "gain": jnp.clip(1.0 + 0.18 * jax.random.normal(seeds[4], (D,), jnp.float32), 0.1, 1.9),
        "w_proj": noise(seeds[5], (OWNERS, D, SLICE), D ** -0.5, 0.15625, ((0, 8),)),
        "cotangent": noise(seeds[6], (PACKS, PACK, INNER), 1.0, 6.0, ((0, 8), (1, 4))),
    }


eps = 1e-05
highest = lax.Precision.HIGHEST

def silu_slope(pre_value):
    sig_value = jax.nn.sigmoid(pre_value)
    return sig_value * (1.0 + pre_value * (1.0 - sig_value))

def visible_mask(query_pos, key_pos, hist_ends, hist_reach):
    query_hist = lax.optimization_barrier(jnp.sum((query_pos[:, None] >= hist_ends[None, :]).astype(jnp.int32), axis=1))
    key_hist = lax.optimization_barrier(jnp.sum((key_pos[:, None] >= hist_ends[None, :]).astype(jnp.int32), axis=1))
    hist_hot = query_hist[:, None] == jnp.arange(hist_ends.shape[0], dtype=jnp.int32)[None, :]
    reach_limit = lax.optimization_barrier(jnp.sum(jnp.where(hist_hot, hist_reach[None, :], 0), axis=1))
    same_hist = query_hist[:, None] == key_hist[None, :]
    causal = (key_pos[None, :] <= query_pos[:, None]) & (key_pos[None, :] >= 0)
    near_block = query_pos[:, None] // MB - key_pos[None, :] // MB <= reach_limit[:, None]
    return same_hist & causal & near_block

def split_heads(matrix):
    return matrix.reshape(matrix.shape[0], HEADS, HD)

def pack_layer(packed):
    gate_u, values, queries, keys_in, cotan, lengths_row, reach_row = packed
    hist_ends = jnp.cumsum(lengths_row).astype(jnp.int32)
    pad_rows = WIN * MB
    window_rows = (WIN + 1) * MB
    block_count = PACK // MB
    score_scale = HD ** (-0.5)
    zero_rows = jnp.zeros((pad_rows, INNER), keys_in.dtype)
    keys_pad = jnp.concatenate([zero_rows, keys_in], axis=0)
    values_pad = jnp.concatenate([zero_rows, values], axis=0)

    def tile_parts(block_number):
        row_start = block_number * MB
        query_tile = split_heads(lax.dynamic_slice_in_dim(queries, row_start, MB, 0)).astype(jnp.float32)
        key_tile = split_heads(lax.dynamic_slice_in_dim(keys_pad, row_start, window_rows, 0)).astype(jnp.float32)
        value_tile = split_heads(lax.dynamic_slice_in_dim(values_pad, row_start, window_rows, 0)).astype(jnp.float32)
        query_pos = row_start + jnp.arange(MB, dtype=jnp.int32)
        key_pos = row_start - pad_rows + jnp.arange(window_rows, dtype=jnp.int32)
        mask_tile = visible_mask(query_pos, key_pos, hist_ends, reach_row)
        scores = jnp.einsum('qhd,khd->hqk', query_tile, key_tile, precision=highest) * score_scale
        weight = jnp.where(mask_tile[None], jax.nn.silu(scores), 0.0).astype(jnp.bfloat16)
        weight_f = lax.optimization_barrier(weight).astype(jnp.float32)
        return (query_tile, key_tile, value_tile, mask_tile, scores, weight_f)

    def forward_tile(block_number):
        parts = tile_parts(block_number)
        mixed_tile = jnp.einsum('hqk,khd->qhd', parts[5], parts[2], precision=highest)
        return mixed_tile.reshape(MB, INNER)
    mixed = lax.map(forward_tile, jnp.arange(block_count, dtype=jnp.int32)).reshape(PACK, INNER)
    row_scale = lax.rsqrt(lax.optimization_barrier(jnp.mean(mixed * mixed, axis=1, keepdims=True)) + eps)
    normed_mix = mixed * row_scale
    gate_f = gate_u.astype(jnp.float32)
    output = (gate_f * normed_mix).astype(jnp.bfloat16)
    cotan_f = cotan.astype(jnp.float32)
    grad_gate = cotan_f * normed_mix
    grad_norm = cotan_f * gate_f
    grad_mixed = (row_scale * (grad_norm - normed_mix * lax.optimization_barrier(jnp.mean(grad_norm * normed_mix, axis=1, keepdims=True)))).astype(jnp.bfloat16)
    grad_mixed_f = lax.optimization_barrier(grad_mixed).astype(jnp.float32)

    def backward_tile(carry, block_number):
        grad_keys_pad, grad_values_pad = carry
        query_tile, key_tile, value_tile, mask_tile, scores, weight_f = tile_parts(block_number)
        row_start = block_number * MB
        grad_tile = split_heads(lax.dynamic_slice_in_dim(grad_mixed_f, row_start, MB, 0))
        grad_att = jnp.einsum('qhd,khd->hqk', grad_tile, value_tile, precision=highest)
        grad_score = jnp.where(mask_tile[None], grad_att * silu_slope(scores), 0.0).astype(jnp.bfloat16)
        grad_score = lax.optimization_barrier(grad_score).astype(jnp.float32)
        grad_query_tile = jnp.einsum('hqk,khd->qhd', grad_score, key_tile, precision=highest) * score_scale
        grad_key_tile = jnp.einsum('hqk,qhd->khd', grad_score, query_tile, precision=highest) * score_scale
        grad_value_tile = jnp.einsum('hqk,qhd->khd', weight_f, grad_tile, precision=highest)
        old_keys = lax.dynamic_slice_in_dim(grad_keys_pad, row_start, window_rows, 0)
        grad_keys_pad = lax.dynamic_update_slice_in_dim(grad_keys_pad, old_keys + grad_key_tile.reshape(window_rows, INNER), row_start, 0)
        old_values = lax.dynamic_slice_in_dim(grad_values_pad, row_start, window_rows, 0)
        grad_values_pad = lax.dynamic_update_slice_in_dim(grad_values_pad, old_values + grad_value_tile.reshape(window_rows, INNER), row_start, 0)
        return ((grad_keys_pad, grad_values_pad), grad_query_tile.reshape(MB, INNER))
    zero_grad = jnp.zeros((PACK + pad_rows, INNER), jnp.float32)
    carried, grad_queries = lax.scan(backward_tile, (zero_grad, zero_grad), jnp.arange(block_count, dtype=jnp.int32))
    grad_proj = jnp.concatenate([grad_gate, carried[1][pad_rows:], grad_queries.reshape(PACK, INNER), carried[0][pad_rows:]], axis=1).astype(jnp.bfloat16)
    return (output, grad_proj)

def reference(events, scenario, lengths, offsets, gain, w_proj, cotangent):
    tokens = PACKS * PACK
    events_f = events.reshape(tokens, D).astype(jnp.float32)
    row_inv = lax.rsqrt(lax.optimization_barrier(jnp.mean(events_f * events_f, axis=1, keepdims=True)) + eps)
    normed = (events_f * row_inv * gain[None, :]).astype(jnp.bfloat16)
    weights = w_proj.reshape(SCEN, SLICES, D, SLICE).transpose(0, 2, 1, 3).reshape(SCEN, D, PROJ)
    scen_ids = scenario.reshape(tokens)
    block_count = tokens // ROWS
    scen_hot = (scen_ids.reshape(block_count, ROWS)[:, :, None] == jnp.arange(SCEN, dtype=jnp.int32)[None, None, :]).astype(jnp.int32)
    slot_rank = lax.optimization_barrier(jnp.sum((jnp.cumsum(scen_hot, axis=1) - 1) * scen_hot, axis=2)).reshape(tokens).astype(jnp.int32)
    slot_index = jnp.arange(tokens, dtype=jnp.int32) // ROWS * CAP + slot_rank

    def through(row_values, matrices):
        sectioning = jnp.zeros((SCEN, block_count * CAP, row_values.shape[1]), row_values.dtype).at[scen_ids, slot_index].set(row_values)
        sectioning = lax.optimization_barrier(sectioning)

        def apply_one(pair):
            return jnp.dot(pair[0].astype(jnp.float32), pair[1].astype(jnp.float32), precision=highest)
        result = lax.map(apply_one, (sectioning, matrices))
        return result[scen_ids, slot_index]
    pre_act = through(normed, weights)
    projected = jax.nn.silu(pre_act).astype(jnp.bfloat16).reshape(PACKS, PACK, PROJ)
    pieces = (projected[:, :, :INNER], projected[:, :, INNER:2 * INNER], projected[:, :, 2 * INNER:3 * INNER], projected[:, :, 3 * INNER:], cotangent, lengths, offsets)
    output, grad_proj = lax.map(pack_layer, pieces)
    grad_pre = (grad_proj.reshape(tokens, PROJ).astype(jnp.float32) * silu_slope(pre_act)).astype(jnp.bfloat16)
    grad_normed = through(grad_pre, jnp.swapaxes(weights, 1, 2))
    scaled = grad_normed * gain[None, :]
    normed_f = events_f * row_inv
    grad_events = row_inv * (scaled - normed_f * lax.optimization_barrier(jnp.mean(scaled * normed_f, axis=1, keepdims=True)))
    return (output, grad_events.astype(jnp.bfloat16).reshape(PACKS, PACK, D))
```

```python
import functools

import jax
import jax.numpy as jnp
from jax import lax
from jax.experimental import pallas as pl
from jax.experimental.pallas import tpu as pltpu
from jax.sharding import PartitionSpec as P

HEADS = 6
HD = 128
SCEN = 8
MB = 128
CAP = 20
REACH = 4

MAIN = 16
EXTRA = CAP - MAIN
FOLD = MAIN // EXTRA

eps = 1e-05
f32 = jnp.float32
bf16 = jnp.bfloat16
NT = (((1,), (1,)), ((), ()))


def whole(count):
    return [pl.BlockSpec(memory_space=pltpu.VMEM) for _ in range(count)]


def call(kernel, outs, operands, name, flops=1 << 24, smem=0, limit=None):
    specs = whole(len(operands) - smem) + [
        pl.BlockSpec(memory_space=pltpu.SMEM) for _ in range(smem)
    ]
    moved = sum(o.size * o.dtype.itemsize for o in list(outs) + list(operands))
    return pl.pallas_call(
        kernel,
        out_shape=tuple(outs),
        in_specs=specs,
        out_specs=tuple(whole(len(outs))),
        name=name,
        cost_estimate=pl.CostEstimate(flops=flops, bytes_accessed=moved, transcendentals=0),
        compiler_params=pltpu.CompilerParams(vmem_limit_bytes=limit or (24 << 20)),
    )(*operands)


def shape(dims, dtype):
    return jax.ShapeDtypeStruct(dims, dtype)


def dot(a, b):
    return jnp.dot(a, b, preferred_element_type=f32)


def dot_nt(a, b):
    return lax.dot_general(a, b, NT, preferred_element_type=f32)


def sigmoid(v):
    return 0.5 * jnp.tanh(0.5 * v) + 0.5


def iotas(rows, cols):
    return (
        lax.broadcasted_iota(jnp.int32, (rows, cols), 0),
        lax.broadcasted_iota(jnp.int32, (rows, cols), 1),
    )


def hot(condition):
    return jnp.where(condition, 1.0, 0.0).astype(bf16)


def slot_matrices(scen_row, by_slot):
    rows = scen_row.shape[1]
    down, along = iotas(rows, rows)
    scen_b = jnp.broadcast_to(scen_row.astype(f32), (rows, rows))
    scen_col = jnp.sum(jnp.where(down == along, scen_b, 0.0), axis=1, keepdims=True)
    same = scen_b == scen_col
    if by_slot:
        scen = scen_row.astype(f32)
        rank = jnp.sum(jnp.where(same & (down < along), 1.0, 0.0), axis=0, keepdims=True)
        down, along = iotas(SCEN * MAIN, rows)
        slot = down.astype(f32)
    else:
        scen = scen_col
        rank = jnp.sum(jnp.where(same & (along < down), 1.0, 0.0), axis=1, keepdims=True)
        down, along = iotas(rows, SCEN * MAIN)
        slot = along.astype(f32)
    main = jnp.where(rank < MAIN, scen * MAIN + rank, -1.0)
    out = [hot(slot == main)]
    for piece in range(FOLD):
        extra = jnp.where(rank >= MAIN, scen * MAIN + EXTRA * piece + (rank - MAIN), -1.0)
        out.append(hot(slot == extra))
    return out


def to_slots(matrices, value, wire_ref):
    cols = value.shape[1]
    piece = cols // FOLD
    wire_ref[:, :cols] = dot(matrices[0], value).astype(bf16)
    extra = dot(matrices[1], value[:, :piece])
    for part in range(1, FOLD):
        extra = extra + dot(matrices[1 + part], value[:, part * piece : (part + 1) * piece])
    wire_ref[:, cols:] = extra.astype(bf16)


def from_slots(matrices, wire_ref):
    cols = wire_ref.shape[1] * FOLD // (FOLD + 1)
    piece = cols // FOLD
    extra = wire_ref[:, cols:]
    out = []
    for part in range(FOLD):
        left = jnp.concatenate([matrices[0], matrices[1 + part]], axis=1)
        right = jnp.concatenate([wire_ref[:, part * piece : (part + 1) * piece], extra], axis=0)
        out.append(dot(left, right))
    return jnp.concatenate(out, axis=1)


def parts_to_slots(slots_ref, parts, wires):
    matrices = [slots_ref[i] for i in range(1 + FOLD)]
    if len(wires) == 1:
        parts = [jnp.concatenate(parts, axis=1)]
    for part, wire_ref in zip(parts, wires):
        to_slots(matrices, part, wire_ref)


def extra_matrix(count, part, by_row):
    if by_row:
        down, along = iotas(count * EXTRA, count * MAIN)
    else:
        along, down = iotas(count * MAIN, count * EXTRA)
    group = sum((down >= EXTRA * i).astype(jnp.int32) for i in range(1, count))
    return hot(along == down + group * (MAIN - EXTRA) + EXTRA * part)


def unfold(wire_ref):
    count = wire_ref.shape[0] // MAIN
    cols = wire_ref.shape[1] * FOLD // (FOLD + 1)
    extra = wire_ref[:, cols:]
    pieces = [dot(extra_matrix(count, part, True), extra) for part in range(FOLD)]
    return jnp.concatenate([wire_ref[:, :cols], jnp.concatenate(pieces, axis=1).astype(bf16)], axis=0)


def fold(value, wire_ref):
    rows, cols = wire_ref.shape[0], value.shape[1]
    count = rows // MAIN
    piece = cols // FOLD
    wire_ref[:, :cols] = value[:rows]
    extra = sum(
        dot(extra_matrix(count, part, False), value[rows:, part * piece : (part + 1) * piece])
        for part in range(FOLD)
    )
    wire_ref[:, cols:] = extra.astype(bf16)


def enter_kernel(events_ref, gain_ref, scen_ref, wire_ref, slots_ref):
    events = events_ref[...].astype(f32)
    row_inv = lax.rsqrt(jnp.mean(events * events, axis=1, keepdims=True) + eps)
    normed = (events * row_inv * gain_ref[...]).astype(bf16)
    matrices = slot_matrices(scen_ref[...], True)
    for i, matrix in enumerate(matrices):
        slots_ref[i] = matrix
    to_slots(matrices, normed, wire_ref)


def history_of(pos, ends):
    return sum((pos >= end).astype(jnp.int32) for end in ends)


def limit_of(history, limits):
    return sum(jnp.where(history == i, limit, 0) for i, limit in enumerate(limits))


def mask_kernel(blocks, scen_ref, lengths_ref, offsets_ref, first_ref, rows_ref, see_ref, seen_ref):
    for i, matrix in enumerate(slot_matrices(scen_ref[...], False)):
        rows_ref[i] = matrix
    rows = see_ref.shape[0]
    ends, total = [], 0
    for i in range(lengths_ref.shape[1]):
        total = total + lengths_ref[0, i]
        ends.append(total)
    limits = [offsets_ref[0, i] for i in range(offsets_ref.shape[1])]
    first = first_ref[0]
    shift = MB.bit_length() - 1

    def visible(query, key):
        query_hist, key_hist = history_of(query, ends), history_of(key, ends)
        near = (query >> shift) - (key >> shift) <= limit_of(query_hist, limits)
        return jnp.where((query_hist == key_hist) & (key <= query) & (key >= 0) & near, 1.0, 0.0)

    down = lax.broadcasted_iota(jnp.int32, (rows, rows), 0)
    along = lax.broadcasted_iota(jnp.int32, (rows, rows), 1)
    for block in range(blocks):
        span = slice(block * rows, (block + 1) * rows)
        see_ref[:, span] = visible(first + down, first - block * rows + along)
        seen_ref[:, span] = visible(first + block * rows + along, first + down)


def project_kernel(parts, wire_ref, w_ref, out_ref, slope_ref):
    rows = unfold(wire_ref)
    width = HEADS * HD
    done = []
    for i, part in enumerate(parts):
        pre = dot(rows, w_ref[:, part * width : (part + 1) * width])
        sig = sigmoid(pre)
        slope_ref[:, i * width : (i + 1) * width] = sig * (1.0 + pre * (1.0 - sig))
        done.append((pre * sig).astype(bf16))
    fold(jnp.concatenate(done, axis=1), out_ref)


def rows_kernel(wire_ref, rows_ref, out_ref):
    matrices = [rows_ref[i] for i in range(1 + FOLD)]
    out_ref[...] = from_slots(matrices, wire_ref).astype(bf16)


def head_cols(head, part=0):
    start = (part * HEADS + head) * HD
    return slice(start, start + HD)


def forward_kernel(blocks, see_ref, gq_ref, cotan_ref, *refs):
    pairs, (out_ref, grad_ref, gate_ref, mixed_ref) = refs[:blocks], refs[blocks:]
    rows = gq_ref.shape[0]
    scale = HD ** (-0.5)
    total = jnp.zeros((rows, 1), f32)
    for head in range(HEADS):
        query = gq_ref[:, head_cols(head, 1)]
        mixed = jnp.zeros((rows, HD), f32)
        for block in range(blocks):
            score = dot_nt(query, pairs[block][:, head_cols(head, 1)]) * scale
            weight = score * sigmoid(score) * see_ref[:, block * rows : (block + 1) * rows]
            mixed = mixed + dot(weight.astype(bf16), pairs[block][:, head_cols(head)])
        mixed_ref[:, head_cols(head)] = mixed
        total = total + jnp.sum(mixed * mixed, axis=1, keepdims=True)
    width = HEADS * HD
    row_scale = lax.rsqrt(total / width + eps)
    normed = mixed_ref[...] * row_scale
    gate = gq_ref[:, :width].astype(f32)
    cotan = cotan_ref[...].astype(f32)
    grad_norm = cotan * gate
    mean = jnp.mean(grad_norm * normed, axis=1, keepdims=True)
    grad_ref[...] = (row_scale * (grad_norm - normed * mean)).astype(bf16)
    out_ref[...] = (gate * normed).astype(bf16)
    gate_ref[...] = (cotan * normed).astype(bf16)


def slope_of(score):
    sig = sigmoid(score)
    return sig, sig * (1.0 + score * (1.0 - sig))


def query_kernel(blocks, see_ref, gq_ref, grad_ref, gate_ref, slots_ref, *refs):
    pairs, wires = refs[:blocks], refs[blocks:]
    rows = gq_ref.shape[0]
    scale = HD ** (-0.5)
    done = []
    for head in range(HEADS):
        query = gq_ref[:, head_cols(head, 1)]
        grad = grad_ref[:, head_cols(head)]
        grad_query = jnp.zeros((rows, HD), f32)
        for block in range(blocks):
            key = pairs[block][:, head_cols(head, 1)]
            score = dot_nt(query, key) * scale
            _, slope = slope_of(score)
            att = dot_nt(grad, pairs[block][:, head_cols(head)])
            grad_score = att * slope * see_ref[:, block * rows : (block + 1) * rows]
            grad_query = grad_query + dot(grad_score.astype(bf16), key)
        done.append((grad_query * scale).astype(bf16))
    parts_to_slots(slots_ref, [gate_ref[...], jnp.concatenate(done, axis=1)], wires)


def key_kernel(blocks, seen_ref, pair_ref, slots_ref, *refs):
    queries, grads, wires = refs[:blocks], refs[blocks : 2 * blocks], refs[2 * blocks :]
    rows = pair_ref.shape[0]
    scale = HD ** (-0.5)
    grad_keys, grad_values = [], []
    for head in range(HEADS):
        key = pair_ref[:, head_cols(head, 1)]
        value = pair_ref[:, head_cols(head)]
        grad_key = jnp.zeros((rows, HD), f32)
        grad_value = jnp.zeros((rows, HD), f32)
        for block in range(blocks):
            mask = seen_ref[:, block * rows : (block + 1) * rows]
            query = queries[block][:, head_cols(head, 1 if block == 0 else 0)]
            grad = grads[block][:, head_cols(head)]
            score = dot_nt(key, query) * scale
            sig, slope = slope_of(score)
            weight = score * sig * mask
            grad_score = dot_nt(value, grad) * slope * mask
            grad_key = grad_key + dot(grad_score.astype(bf16), query)
            grad_value = grad_value + dot(weight.astype(bf16), grad)
        grad_keys.append((grad_key * scale).astype(bf16))
        grad_values.append(grad_value.astype(bf16))
    parts = [jnp.concatenate(one, axis=1) for one in (grad_values, grad_keys)]
    parts_to_slots(slots_ref, parts, wires)


def owner_term(parts, wire_ref, slope_ref, w_ref):
    width = HEADS * HD
    grad_pre = (unfold(wire_ref).astype(f32) * slope_ref[...]).astype(bf16)
    term = None
    for i, part in enumerate(parts):
        one = dot_nt(
            grad_pre[:, i * width : (i + 1) * width], w_ref[:, part * width : (part + 1) * width]
        )
        term = one if term is None else term + one
    return term


def term_kernel(parts, wire_ref, slope_ref, w_ref, out_ref):
    out_ref[...] = owner_term(parts, wire_ref, slope_ref, w_ref)


def last_term_kernel(parts, wire_ref, slope_ref, w_ref, *refs):
    term = owner_term(parts, wire_ref, slope_ref, w_ref)
    for other_ref in refs[:-1]:
        term = term + other_ref[...]
    fold(term.astype(bf16), refs[-1])


def leave_kernel(rows_ref, events_ref, gain_ref, *refs):
    wires, out_ref = refs[:-1], refs[-1]
    matrices = [rows_ref[i] for i in range(1 + FOLD)]
    scaled = sum(from_slots(matrices, wire_ref) for wire_ref in wires) * gain_ref[...]
    events = events_ref[...].astype(f32)
    row_inv = lax.rsqrt(jnp.mean(events * events, axis=1, keepdims=True) + eps)
    normed = events * row_inv
    mean = jnp.mean(scaled * normed, axis=1, keepdims=True)
    out_ref[...] = (row_inv * (scaled - normed * mean)).astype(bf16)


def exchange(wire):
    blocks = wire.reshape(-1, MAIN, wire.shape[1])
    done = lax.all_to_all(blocks, "user", split_axis=0, concat_axis=0, tiled=True)
    return done.reshape(wire.shape)


def shifted(block, distance):
    devices = range(lax.axis_size("seq"))
    route = [(i - distance, i) for i in devices if i - distance in devices]
    return lax.ppermute(block, "seq", route)


def wires_of(split, boxes):
    if split == 1:
        return boxes[0]
    cols = boxes[0].shape[1]
    return jnp.stack([box.reshape(SCEN, MAIN, cols) for box in boxes], axis=1).reshape(-1, cols)


def slices_of(split, box):
    if split == 1:
        return [box]
    cols = box.shape[1]
    blocks = box.reshape(SCEN, split, MAIN, cols)
    return [blocks[:, i].reshape(-1, cols) for i in range(split)]


def shards(events, scenario, lengths, offsets, gain, w_proj, cotangent):
    n_seq = lax.axis_size("seq")
    n_user = lax.axis_size("user")
    split = n_user // SCEN
    rows, feats = events.shape[1:]
    width = HEADS * HD
    longest = n_seq * rows // 2
    reach = min(REACH, n_seq - 1, (longest - 2) // rows + 1)
    blocks = reach + 1
    slots = SCEN * MAIN

    def wire(senders, cols):
        return shape((senders * MAIN, cols * (FOLD + 1) // FOLD), bf16)

    matrices = shape((1 + FOLD, rows, slots), bf16)
    events, w_local, cotan = events[0], w_proj[0], cotangent[0]
    gain = gain[None]
    first = (lax.axis_index("seq") * rows).astype(jnp.int32)[None]

    outbox, to_slot = call(
        enter_kernel, [wire(SCEN, feats), matrices], [events, gain, scenario], "enter"
    )
    inbound = exchange(wires_of(split, [outbox] * split))
    to_row, see, seen = call(
        functools.partial(mask_kernel, blocks),
        [matrices] + [shape((rows, blocks * rows), f32)] * 2,
        [scenario, lengths, offsets, first],
        "masks",
        smem=3,
    )

    def project(parts, name):
        cols = len(parts) * width
        return call(
            functools.partial(project_kernel, parts),
            [wire(n_user, cols), shape((n_user * CAP, cols), f32)],
            [inbound, w_local],
            name,
        )

    def rows_of(box, name):
        cols = box.shape[1] * FOLD // (FOLD + 1)
        return call(rows_kernel, [shape((rows, cols), bf16)], [box, to_row], name)[0]

    together = split == 1
    if together:
        pair_parts, query_parts = (1, 3), (0, 2)
        pair_box, pair_slope = project(pair_parts, "pair")
        pair_back = exchange(pair_box)
        query_box, query_slope = project(query_parts, "query")
        pair_own = rows_of(pair_back, "pairs")
        pairs = [pair_own] + [shifted(pair_own, d) for d in range(1, blocks)]
        gq = rows_of(exchange(query_box), "queries")
    else:
        box, slope = project((0,), "all")
        gate, value, query, key = [
            rows_of(part, "part") for part in slices_of(split, exchange(box))
        ]
        pair_own = jnp.concatenate([value, key], axis=1)
        gq = jnp.concatenate([gate, query], axis=1)
        pairs = [pair_own] + [shifted(pair_own, d) for d in range(1, blocks)]
    query_own = gq[:, width:]
    queries = [gq] + [shifted(query_own, -d) for d in range(1, blocks)]
    half = shape((rows, width), bf16)
    output, grad_own, grad_gate, _ = call(
        functools.partial(forward_kernel, blocks),
        [half, half, half, shape((rows, width), f32)],
        [see, gq, cotan] + pairs,
        "forward",
    )
    grads = [grad_own] + [shifted(grad_own, -d) for d in range(1, blocks)]
    boxes = [wire(SCEN, 2 * width)] if together else [wire(SCEN, width)] * 2
    query_grad = call(
        functools.partial(query_kernel, blocks),
        boxes,
        [see, gq, grad_own, grad_gate, to_slot] + pairs,
        "query_grad",
    )
    if together:
        query_grad = exchange(query_grad[0])
    pair_grad = call(
        functools.partial(key_kernel, blocks),
        boxes,
        [seen, pair_own, to_slot] + queries + grads,
        "pair_grad",
    )
    term = shape((n_user * CAP, feats), f32)
    if together:
        pair_grad = exchange(pair_grad[0])
        (query_term,) = call(
            functools.partial(term_kernel, query_parts),
            [term],
            [query_grad, query_slope, w_local],
            "term",
        )
        last_parts, last = pair_parts, [pair_grad, pair_slope, w_local, query_term]
    else:
        order = [query_grad[0], pair_grad[0], query_grad[1], pair_grad[1]]
        last_parts, last = (0,), [exchange(wires_of(split, order)), slope, w_local]
    (term_box,) = call(
        functools.partial(last_term_kernel, last_parts), [wire(n_user, feats)], last, "last_term"
    )
    (grad_events,) = call(
        leave_kernel,
        [shape((rows, feats), bf16)],
        [to_row, events, gain] + slices_of(split, exchange(term_box)),
        "leave",
    )
    return output[None], grad_events[None]


def solution(mesh):
    placed = (
        P("user", "seq", None),
        P("user", "seq"),
        P("user", None),
        P("user", None),
        P(),
        P("user", None, None),
        P("user", "seq", None),
    )
    return jax.shard_map(
        shards,
        mesh=mesh,
        in_specs=placed,
        out_specs=(P("user", "seq", None), P("user", "seq", None)),
        check_vma=False,
    )
```

```python
import functools

import jax
import jax.numpy as jnp
from jax import lax
from jax.experimental import pallas as pl
from jax.experimental.pallas import tpu as pltpu
from jax.sharding import PartitionSpec as P

HEADS = 6
HD = 128
SCEN = 8
MB = 128
CAP = 20
REACH = 4

MAIN = 16
EXTRA = CAP - MAIN
FOLD = MAIN // EXTRA

eps = 1e-05
f32 = jnp.float32
bf16 = jnp.bfloat16
NT = (((1,), (1,)), ((), ()))


def whole(count):
    return [pl.BlockSpec(memory_space=pltpu.VMEM) for _ in range(count)]


def call(kernel, outs, operands, name, flops=1 << 24, smem=0, limit=None):
    specs = whole(len(operands) - smem) + [
        pl.BlockSpec(memory_space=pltpu.SMEM) for _ in range(smem)
    ]
    moved = sum(o.size * o.dtype.itemsize for o in list(outs) + list(operands))
    return pl.pallas_call(
        kernel,
        out_shape=tuple(outs),
        in_specs=specs,
        out_specs=tuple(whole(len(outs))),
        name=name,
        cost_estimate=pl.CostEstimate(flops=flops, bytes_accessed=moved, transcendentals=0),
        compiler_params=pltpu.CompilerParams(vmem_limit_bytes=limit or (24 << 20)),
    )(*operands)


def shape(dims, dtype):
    return jax.ShapeDtypeStruct(dims, dtype)


def dot(a, b):
    return jnp.dot(a, b, preferred_element_type=f32)


def dot_nt(a, b):
    return lax.dot_general(a, b, NT, preferred_element_type=f32)


def sigmoid(v):
    return 0.5 * jnp.tanh(0.5 * v) + 0.5


def iotas(rows, cols):
    return (
        lax.broadcasted_iota(jnp.int32, (rows, cols), 0),
        lax.broadcasted_iota(jnp.int32, (rows, cols), 1),
    )


def hot(condition):
    return jnp.where(condition, 1.0, 0.0).astype(bf16)


def load(refs, cols):
    parts = [ref[:, cols] for ref in refs]
    return parts[0] if len(parts) == 1 else jnp.concatenate(parts, axis=0)


def store(refs, cols, value):
    rows = refs[0].shape[0]
    for i, ref in enumerate(refs):
        ref[:, cols] = value[i * rows : (i + 1) * rows]


def main_cols(refs):
    return refs[0].shape[1] * FOLD // (FOLD + 1)


def slot_matrices(scen_row, by_slot):
    rows = scen_row.shape[1]
    down, along = iotas(rows, rows)
    scen_b = jnp.broadcast_to(scen_row.astype(f32), (rows, rows))
    scen_col = jnp.sum(jnp.where(down == along, scen_b, 0.0), axis=1, keepdims=True)
    same = scen_b == scen_col
    if by_slot:
        scen = scen_row.astype(f32)
        rank = jnp.sum(jnp.where(same & (down < along), 1.0, 0.0), axis=0, keepdims=True)
        down, along = iotas(SCEN * MAIN, rows)
        slot = down.astype(f32)
    else:
        scen = scen_col
        rank = jnp.sum(jnp.where(same & (along < down), 1.0, 0.0), axis=1, keepdims=True)
        down, along = iotas(rows, SCEN * MAIN)
        slot = along.astype(f32)
    main = jnp.where(rank < MAIN, scen * MAIN + rank, -1.0)
    out = [hot(slot == main)]
    for piece in range(FOLD):
        extra = jnp.where(rank >= MAIN, scen * MAIN + EXTRA * piece + (rank - MAIN), -1.0)
        out.append(hot(slot == extra))
    return out


def to_slots(matrices, value, refs):
    cols = value.shape[1]
    piece = cols // FOLD
    store(refs, slice(0, cols), dot(matrices[0], value).astype(bf16))
    extra = dot(matrices[1], value[:, :piece])
    for part in range(1, FOLD):
        extra = extra + dot(matrices[1 + part], value[:, part * piece : (part + 1) * piece])
    store(refs, slice(cols, cols + piece), extra.astype(bf16))


def from_slots(matrices, refs):
    cols = main_cols(refs)
    piece = cols // FOLD
    extra = load(refs, slice(cols, cols + piece))
    out = []
    for part in range(FOLD):
        left = jnp.concatenate([matrices[0], matrices[1 + part]], axis=1)
        right = jnp.concatenate([load(refs, slice(part * piece, (part + 1) * piece)), extra], axis=0)
        out.append(dot(left, right))
    return jnp.concatenate(out, axis=1)


def parts_to_slots(slots_ref, parts, wires):
    matrices = [slots_ref[i] for i in range(1 + FOLD)]
    if len(wires) == 1:
        parts = [jnp.concatenate(parts, axis=1)]
    for part, refs in zip(parts, wires):
        to_slots(matrices, part, refs)


def extra_matrix(count, part, by_row):
    if by_row:
        down, along = iotas(count * EXTRA, count * MAIN)
    else:
        along, down = iotas(count * MAIN, count * EXTRA)
    group = sum((down >= EXTRA * i).astype(jnp.int32) for i in range(1, count))
    return hot(along == down + group * (MAIN - EXTRA) + EXTRA * part)


def unfold(refs):
    count = sum(ref.shape[0] for ref in refs) // MAIN
    cols = main_cols(refs)
    extra = load(refs, slice(cols, cols + cols // FOLD))
    pieces = [dot(extra_matrix(count, part, True), extra) for part in range(FOLD)]
    extra = jnp.concatenate(pieces, axis=1).astype(bf16)
    return jnp.concatenate([load(refs, slice(0, cols)), extra], axis=0)


def fold(value, refs):
    rows, cols = sum(ref.shape[0] for ref in refs), value.shape[1]
    count = rows // MAIN
    piece = cols // FOLD
    store(refs, slice(0, cols), value[:rows])
    extra = sum(
        dot(extra_matrix(count, part, False), value[rows:, part * piece : (part + 1) * piece])
        for part in range(FOLD)
    )
    store(refs, slice(cols, cols + piece), extra.astype(bf16))


def own_scenarios(scen_ref, direct):
    return scen_ref[...] ^ lax.axis_index("user") if direct else scen_ref[...]


def enter_kernel(direct, events_ref, gain_ref, scen_ref, slots_ref, *refs):
    events = events_ref[...].astype(f32)
    row_inv = lax.rsqrt(jnp.mean(events * events, axis=1, keepdims=True) + eps)
    normed = (events * row_inv * gain_ref[...]).astype(bf16)
    matrices = slot_matrices(own_scenarios(scen_ref, direct), True)
    for i, matrix in enumerate(matrices):
        slots_ref[i] = matrix
    to_slots(matrices, normed, refs)


def history_of(pos, ends):
    return sum((pos >= end).astype(jnp.int32) for end in ends)


def limit_of(history, limits):
    return sum(jnp.where(history == i, limit, 0) for i, limit in enumerate(limits))


def mask_kernel(direct, blocks, scen_ref, lengths_ref, offsets_ref, rows_ref, see_ref, seen_ref):
    for i, matrix in enumerate(slot_matrices(own_scenarios(scen_ref, direct), False)):
        rows_ref[i] = matrix
    rows = see_ref.shape[0]
    ends, total = [], 0
    for i in range(lengths_ref.shape[1]):
        total = total + lengths_ref[0, i]
        ends.append(total)
    limits = [offsets_ref[0, i] for i in range(offsets_ref.shape[1])]
    first = lax.axis_index("seq") * rows
    shift = MB.bit_length() - 1

    def visible(query, key):
        query_hist, key_hist = history_of(query, ends), history_of(key, ends)
        near = (query >> shift) - (key >> shift) <= limit_of(query_hist, limits)
        return jnp.where((query_hist == key_hist) & (key <= query) & (key >= 0) & near, 1.0, 0.0)

    down = lax.broadcasted_iota(jnp.int32, (rows, rows), 0)
    along = lax.broadcasted_iota(jnp.int32, (rows, rows), 1)
    for block in range(blocks):
        span = slice(block * rows, (block + 1) * rows)
        see_ref[:, span] = visible(first + down, first - block * rows + along)
        seen_ref[:, span] = visible(first + block * rows + along, first + down)


def project_kernel(count, parts, w_ref, *refs):
    ins, outs, slope_ref = refs[:count], refs[count : 2 * count], refs[2 * count]
    rows = unfold(ins)
    width = HEADS * HD
    done = []
    for i, part in enumerate(parts):
        pre = dot(rows, w_ref[:, part * width : (part + 1) * width])
        sig = sigmoid(pre)
        slope_ref[:, i * width : (i + 1) * width] = sig * (1.0 + pre * (1.0 - sig))
        done.append((pre * sig).astype(bf16))
    fold(jnp.concatenate(done, axis=1), outs)


def rows_kernel(rows_ref, *refs):
    matrices = [rows_ref[i] for i in range(1 + FOLD)]
    refs[-1][...] = from_slots(matrices, refs[:-1]).astype(bf16)


def head_cols(head, part=0):
    start = (part * HEADS + head) * HD
    return slice(start, start + HD)


def forward_kernel(blocks, see_ref, gq_ref, cotan_ref, *refs):
    pairs, (out_ref, grad_ref, gate_ref, mixed_ref) = refs[:blocks], refs[blocks:]
    rows = gq_ref.shape[0]
    scale = HD ** (-0.5)
    total = jnp.zeros((rows, 1), f32)
    for head in range(HEADS):
        query = gq_ref[:, head_cols(head, 1)]
        mixed = jnp.zeros((rows, HD), f32)
        for block in range(blocks):
            score = dot_nt(query, pairs[block][:, head_cols(head, 1)]) * scale
            weight = score * sigmoid(score) * see_ref[:, block * rows : (block + 1) * rows]
            mixed = mixed + dot(weight.astype(bf16), pairs[block][:, head_cols(head)])
        mixed_ref[:, head_cols(head)] = mixed
        total = total + jnp.sum(mixed * mixed, axis=1, keepdims=True)
    width = HEADS * HD
    row_scale = lax.rsqrt(total / width + eps)
    normed = mixed_ref[...] * row_scale
    gate = gq_ref[:, :width].astype(f32)
    cotan = cotan_ref[...].astype(f32)
    grad_norm = cotan * gate
    mean = jnp.mean(grad_norm * normed, axis=1, keepdims=True)
    grad_ref[...] = (row_scale * (grad_norm - normed * mean)).astype(bf16)
    out_ref[...] = (gate * normed).astype(bf16)
    gate_ref[...] = (cotan * normed).astype(bf16)


def slope_of(score):
    sig = sigmoid(score)
    return sig, sig * (1.0 + score * (1.0 - sig))


def wires_out(count, refs):
    return [refs[i : i + count] for i in range(0, len(refs), count)]


def query_kernel(count, blocks, see_ref, gq_ref, grad_ref, gate_ref, slots_ref, *refs):
    pairs, wires = refs[:blocks], wires_out(count, refs[blocks:])
    rows = gq_ref.shape[0]
    scale = HD ** (-0.5)
    done = []
    for head in range(HEADS):
        query = gq_ref[:, head_cols(head, 1)]
        grad = grad_ref[:, head_cols(head)]
        grad_query = jnp.zeros((rows, HD), f32)
        for block in range(blocks):
            key = pairs[block][:, head_cols(head, 1)]
            score = dot_nt(query, key) * scale
            _, slope = slope_of(score)
            att = dot_nt(grad, pairs[block][:, head_cols(head)])
            grad_score = att * slope * see_ref[:, block * rows : (block + 1) * rows]
            grad_query = grad_query + dot(grad_score.astype(bf16), key)
        done.append((grad_query * scale).astype(bf16))
    parts_to_slots(slots_ref, [gate_ref[...], jnp.concatenate(done, axis=1)], wires)


def key_kernel(count, blocks, seen_ref, pair_ref, slots_ref, *refs):
    queries, grads = refs[:blocks], refs[blocks : 2 * blocks]
    wires = wires_out(count, refs[2 * blocks :])
    rows = pair_ref.shape[0]
    scale = HD ** (-0.5)
    grad_keys, grad_values = [], []
    for head in range(HEADS):
        key = pair_ref[:, head_cols(head, 1)]
        value = pair_ref[:, head_cols(head)]
        grad_key = jnp.zeros((rows, HD), f32)
        grad_value = jnp.zeros((rows, HD), f32)
        for block in range(blocks):
            mask = seen_ref[:, block * rows : (block + 1) * rows]
            query = queries[block][:, head_cols(head, 1 if block == 0 else 0)]
            grad = grads[block][:, head_cols(head)]
            score = dot_nt(key, query) * scale
            sig, slope = slope_of(score)
            weight = score * sig * mask
            grad_score = dot_nt(value, grad) * slope * mask
            grad_key = grad_key + dot(grad_score.astype(bf16), query)
            grad_value = grad_value + dot(weight.astype(bf16), grad)
        grad_keys.append((grad_key * scale).astype(bf16))
        grad_values.append(grad_value.astype(bf16))
    parts = [jnp.concatenate(one, axis=1) for one in (grad_values, grad_keys)]
    parts_to_slots(slots_ref, parts, wires)


def owner_term(parts, refs, slope_ref, w_ref):
    width = HEADS * HD
    grad_pre = (unfold(refs).astype(f32) * slope_ref[...]).astype(bf16)
    term = None
    for i, part in enumerate(parts):
        one = dot_nt(
            grad_pre[:, i * width : (i + 1) * width], w_ref[:, part * width : (part + 1) * width]
        )
        term = one if term is None else term + one
    return term


def term_kernel(parts, slope_ref, w_ref, *refs):
    refs[-1][...] = owner_term(parts, refs[:-1], slope_ref, w_ref)


def last_term_kernel(count, parts, slope_ref, w_ref, *refs):
    ins, others, outs = refs[:count], refs[count:-count], refs[-count:]
    term = owner_term(parts, ins, slope_ref, w_ref)
    for other_ref in others:
        term = term + other_ref[...]
    fold(term.astype(bf16), outs)


def leave_kernel(count, rows_ref, events_ref, gain_ref, *refs):
    matrices = [rows_ref[i] for i in range(1 + FOLD)]
    wires = wires_out(count, refs[:-1])
    scaled = sum(from_slots(matrices, wire) for wire in wires) * gain_ref[...]
    events = events_ref[...].astype(f32)
    row_inv = lax.rsqrt(jnp.mean(events * events, axis=1, keepdims=True) + eps)
    normed = events * row_inv
    mean = jnp.mean(scaled * normed, axis=1, keepdims=True)
    refs[-1][...] = (row_inv * (scaled - normed * mean)).astype(bf16)


def exchange(blocks):
    if len(blocks) == 1:
        wire = blocks[0].reshape(-1, MAIN, blocks[0].shape[1])
        done = lax.all_to_all(wire, "user", split_axis=0, concat_axis=0, tiled=True)
        return [done.reshape(blocks[0].shape)]
    count = lax.axis_size("user")
    done = list(blocks)
    for k in range(count - 1, 0, -1):
        done[k] = lax.ppermute(blocks[k], "user", [(i, i ^ k) for i in range(count)])
    return done


def shifted(block, distance):
    devices = range(lax.axis_size("seq"))
    route = [(i - distance, i) for i in devices if i - distance in devices]
    return lax.ppermute(block, "seq", route)


def wires_of(split, boxes):
    cols = boxes[0].shape[1]
    return [jnp.stack([box.reshape(SCEN, MAIN, cols) for box in boxes], axis=1).reshape(-1, cols)]


def slices_of(split, box):
    cols = box.shape[1]
    blocks = box.reshape(SCEN, split, MAIN, cols)
    return [blocks[:, i].reshape(-1, cols) for i in range(split)]


def shards(events, scenario, lengths, offsets, gain, w_proj, cotangent):
    n_seq = lax.axis_size("seq")
    n_user = lax.axis_size("user")
    split = n_user // SCEN
    rows, feats = events.shape[1:]
    width = HEADS * HD
    longest = n_seq * rows // 2
    reach = min(REACH, n_seq - 1, (longest - 2) // rows + 1)
    blocks = reach + 1
    direct = split == 1
    senders = SCEN if direct else 1

    def wire(rows, cols):
        count = rows // MAIN if direct else 1
        return [shape((rows // count, cols * (FOLD + 1) // FOLD), bf16)] * count

    slots = wire(SCEN * MAIN, feats)
    matrices = shape((1 + FOLD, rows, SCEN * MAIN), bf16)
    events, w_local, cotan = events[0], w_proj[0], cotangent[0]
    gain = gain[None]

    to_slot, *outbox = call(
        functools.partial(enter_kernel, direct),
        [matrices] + slots,
        [events, gain, scenario],
        "enter",
    )
    inbound = exchange(outbox if direct else wires_of(split, outbox * split))
    to_row, see, seen = call(
        functools.partial(mask_kernel, direct, blocks),
        [matrices] + [shape((rows, blocks * rows), f32)] * 2,
        [scenario, lengths, offsets],
        "masks",
        smem=2,
    )

    def project(parts, name):
        cols = len(parts) * width
        *box, slope = call(
            functools.partial(project_kernel, senders, parts),
            wire(n_user * MAIN, cols) + [shape((n_user * CAP, cols), f32)],
            [w_local] + inbound,
            name,
        )
        return exchange(box), slope

    def rows_of(box, name):
        cols = box[0].shape[1] * FOLD // (FOLD + 1)
        return call(rows_kernel, [shape((rows, cols), bf16)], [to_row] + box, name)[0]

    if direct:
        pair_parts, query_parts = (1, 3), (0, 2)
        pair_back, pair_slope = project(pair_parts, "pair")
        query_back, query_slope = project(query_parts, "query")
        pair_own = rows_of(pair_back, "pairs")
        gq = rows_of(query_back, "queries")
    else:
        (box,), slope = project((0,), "all")
        gate, value, query, key = [rows_of([part], "part") for part in slices_of(split, box)]
        pair_own = jnp.concatenate([value, key], axis=1)
        gq = jnp.concatenate([gate, query], axis=1)
    pairs = [pair_own] + [shifted(pair_own, d) for d in range(1, blocks)]
    query_own = gq[:, width:]
    queries = [gq] + [shifted(query_own, -d) for d in range(1, blocks)]
    half = shape((rows, width), bf16)
    output, grad_own, grad_gate, _ = call(
        functools.partial(forward_kernel, blocks),
        [half, half, half, shape((rows, width), f32)],
        [see, gq, cotan] + pairs,
        "forward",
    )
    grads = [grad_own] + [shifted(grad_own, -d) for d in range(1, blocks)]
    boxes = wire(SCEN * MAIN, 2 * width) if direct else wire(SCEN * MAIN, width) * 2
    query_grad = call(
        functools.partial(query_kernel, senders, blocks),
        boxes,
        [see, gq, grad_own, grad_gate, to_slot] + pairs,
        "query_grad",
    )
    pair_grad = call(
        functools.partial(key_kernel, senders, blocks),
        boxes,
        [seen, pair_own, to_slot] + queries + grads,
        "pair_grad",
    )
    term = shape((n_user * CAP, feats), f32)
    if direct:
        (query_term,) = call(
            functools.partial(term_kernel, query_parts),
            [term],
            [query_slope, w_local] + exchange(query_grad),
            "term",
        )
        last_parts, last = pair_parts, [pair_slope, w_local] + exchange(pair_grad) + [query_term]
    else:
        order = [query_grad[0], pair_grad[0], query_grad[1], pair_grad[1]]
        last_parts, last = (0,), [slope, w_local] + exchange(wires_of(split, order))
    term_box = call(
        functools.partial(last_term_kernel, senders, last_parts),
        wire(n_user * MAIN, feats),
        last,
        "last_term",
    )
    term_back = exchange(term_box)
    (grad_events,) = call(
        functools.partial(leave_kernel, senders),
        [shape((rows, feats), bf16)],
        [to_row, events, gain] + (term_back if direct else slices_of(split, term_back[0])),
        "leave",
    )
    return output[None], grad_events[None]


def solution(mesh):
    placed = (
        P("user", "seq", None),
        P("user", "seq"),
        P("user", None),
        P("user", None),
        P(),
        P("user", None, None),
        P("user", "seq", None),
    )
    return jax.shard_map(
        shards,
        mesh=mesh,
        in_specs=placed,
        out_specs=(P("user", "seq", None), P("user", "seq", None)),
        check_vma=False,
    )
```

```python
import functools

import jax
import jax.numpy as jnp
from jax import lax
from jax.experimental import pallas as pl
from jax.experimental.pallas import tpu as pltpu
from jax.sharding import PartitionSpec as P


HEADS = 6
HD = 128
SCEN = 8
MB = 128
CAP = 20
REACH = 4

MAIN = 16
EXTRA = CAP - MAIN
FOLD = MAIN // EXTRA

VMEM_LIMIT = 24 << 20
VMEM_ALL = 67043328
LANES = 128

eps = 1e-05
f32 = jnp.float32
bf16 = jnp.bfloat16
NT = (((1,), (1,)), ((), ()))


def call(kernel, outs, operands, spaces=(), scratch=(), flops=1 << 24, limit=VMEM_LIMIT):
    spaces = list(spaces) + [pltpu.VMEM] * (len(operands) - len(spaces))
    moved = sum(o.size * o.dtype.itemsize for o in list(outs) + list(operands))
    return pl.pallas_call(
        kernel,
        out_shape=tuple(outs),
        in_specs=[pl.BlockSpec(memory_space=space) for space in spaces],
        out_specs=tuple(pl.BlockSpec(memory_space=pltpu.VMEM) for _ in outs),
        scratch_shapes=list(scratch),
        cost_estimate=pl.CostEstimate(flops=flops, bytes_accessed=moved, transcendentals=0),
        compiler_params=pltpu.CompilerParams(vmem_limit_bytes=limit),
    )(*operands)


def shape(dims, dtype):
    return jax.ShapeDtypeStruct(dims, dtype)


def dot(a, b):
    return jnp.dot(a, b, preferred_element_type=f32)


def dot_nt(a, b):
    return lax.dot_general(a, b, NT, preferred_element_type=f32)


def sigmoid(v):
    return 0.5 * jnp.tanh(0.5 * v) + 0.5


def iotas(rows, cols):
    return (
        lax.broadcasted_iota(jnp.int32, (rows, cols), 0),
        lax.broadcasted_iota(jnp.int32, (rows, cols), 1),
    )


def hot(condition):
    return jnp.where(condition, 1.0, 0.0).astype(bf16)


def load(refs, cols):
    if swapped(refs):
        parts = []
        for i, ref in enumerate(refs[:-1]):
            parts += [ref[:MAIN, cols], refs[-1][i * MAIN : (i + 1) * MAIN, cols]]
    else:
        parts = [ref[:, cols] for ref in refs]
    return parts[0] if len(parts) == 1 else jnp.concatenate(parts, axis=0)


def swapped(refs):
    return len(refs) > 1 and refs[0].shape[0] == 2 * MAIN


def rows_in(refs):
    return 2 * refs[-1].shape[0] if swapped(refs) else sum(ref.shape[0] for ref in refs)


def store(refs, cols, value):
    rows = refs[0].shape[0]
    for i, ref in enumerate(refs):
        ref[:, cols] = value[i * rows : (i + 1) * rows]


def main_cols(refs):
    return refs[0].shape[1] * FOLD // (FOLD + 1)


def slot_matrices(scen_row, by_slot):
    rows = scen_row.shape[1]
    down, along = iotas(rows, rows)
    scen_b = jnp.broadcast_to(scen_row.astype(f32), (rows, rows))
    scen_col = jnp.sum(jnp.where(down == along, scen_b, 0.0), axis=1, keepdims=True)
    same = scen_b == scen_col
    if by_slot:
        scen = scen_row.astype(f32)
        rank = jnp.sum(jnp.where(same & (down < along), 1.0, 0.0), axis=0, keepdims=True)
        down, along = iotas(SCEN * MAIN, rows)
        slot = down.astype(f32)
    else:
        scen = scen_col
        rank = jnp.sum(jnp.where(same & (along < down), 1.0, 0.0), axis=1, keepdims=True)
        down, along = iotas(rows, SCEN * MAIN)
        slot = along.astype(f32)
    main = jnp.where(rank < MAIN, scen * MAIN + rank, -1.0)
    out = [hot(slot == main)]
    for piece in range(FOLD):
        extra = jnp.where(rank >= MAIN, scen * MAIN + EXTRA * piece + (rank - MAIN), -1.0)
        out.append(hot(slot == extra))
    return out


def to_slots(matrices, value, refs):
    cols = value.shape[1]
    piece = cols // FOLD
    store(refs, slice(0, cols), dot(matrices[0], value).astype(bf16))
    extra = dot(matrices[1], value[:, :piece])
    for part in range(1, FOLD):
        extra = extra + dot(matrices[1 + part], value[:, part * piece : (part + 1) * piece])
    store(refs, slice(cols, cols + piece), extra.astype(bf16))


def from_slots(matrices, refs):
    cols = main_cols(refs)
    piece = cols // FOLD
    extra = load(refs, slice(cols, cols + piece))
    out = []
    for part in range(FOLD):
        left = jnp.concatenate([matrices[0], matrices[1 + part]], axis=1)
        right = jnp.concatenate([load(refs, slice(part * piece, (part + 1) * piece)), extra], axis=0)
        out.append(dot(left, right))
    return jnp.concatenate(out, axis=1)


def parts_to_slots(slots_ref, parts, wires):
    matrices = [slots_ref[i] for i in range(1 + FOLD)]
    if len(wires) == 1:
        parts = [jnp.concatenate(parts, axis=1)]
    for part, refs in zip(parts, wires):
        to_slots(matrices, part, refs)


def extra_matrix(count, part, by_row):
    if by_row:
        down, along = iotas(count * EXTRA, count * MAIN)
    else:
        along, down = iotas(count * MAIN, count * EXTRA)
    group = sum((down >= EXTRA * i).astype(jnp.int32) for i in range(1, count))
    return hot(along == down + group * (MAIN - EXTRA) + EXTRA * part)


def unfold(refs):
    count = rows_in(refs) // MAIN
    cols = main_cols(refs)
    extra = load(refs, slice(cols, cols + cols // FOLD))
    pieces = [dot(extra_matrix(count, part, True), extra) for part in range(FOLD)]
    extra = jnp.concatenate(pieces, axis=1).astype(bf16)
    return jnp.concatenate([load(refs, slice(0, cols)), extra], axis=0)


def fold(value, refs):
    rows, cols = sum(ref.shape[0] for ref in refs), value.shape[1]
    count = rows // MAIN
    piece = cols // FOLD
    store(refs, slice(0, cols), value[:rows])
    extra = sum(
        dot(extra_matrix(count, part, False), value[rows:, part * piece : (part + 1) * piece])
        for part in range(FOLD)
    )
    store(refs, slice(cols, cols + piece), extra.astype(bf16))


def own_scenarios(scen_ref, direct):
    return scen_ref[...] ^ lax.axis_index("user") if direct else scen_ref[...]


def gain_of(gain_ref):
    return jnp.concatenate([gain_ref[i : i + 1] for i in range(gain_ref.shape[0])], axis=1)


def enter_kernel(direct, events_hbm, gain_hbm, scen_hbm, slots_ref, *refs):
    events_ref, gain_ref, scen_ref, sems = refs[-4:]
    refs = refs[:-4]
    loads = [
        pltpu.make_async_copy(source, target, sems.at[i])
        for i, (source, target) in enumerate(
            [(events_hbm, events_ref), (gain_hbm, gain_ref), (scen_hbm, scen_ref)]
        )
    ]
    for load_ in loads:
        load_.start()
    for load_ in loads:
        load_.wait()
    events = events_ref[...].astype(f32)
    row_inv = lax.rsqrt(jnp.mean(events * events, axis=1, keepdims=True) + eps)
    normed = (events * row_inv * gain_of(gain_ref)).astype(bf16)
    matrices = slot_matrices(own_scenarios(scen_ref, direct), True)
    for i, matrix in enumerate(matrices):
        slots_ref[i] = matrix
    to_slots(matrices, normed, refs)


def history_of(pos, ends):
    return sum((pos >= end).astype(jnp.int32) for end in ends)


def limit_of(history, limits):
    return sum(jnp.where(history == i, limit, 0) for i, limit in enumerate(limits))


def mask_kernel(direct, blocks, w_hbm, *refs):
    small, (w_ref, rows_ref, see_ref, seen_ref), rest = refs[:3], refs[3:7], refs[7:]
    lengths_ref, offsets_ref, scen_ref, sems = rest
    count = sems.shape[0] - len(small)
    depth = w_ref.shape[0] // count
    loads = [
        pltpu.make_async_copy(
            w_hbm.at[pl.ds(i * depth, depth)], w_ref.at[pl.ds(i * depth, depth)], sems.at[i]
        )
        for i in range(count)
    ]
    first_loads = [
        pltpu.make_async_copy(source, target, sems.at[count + i])
        for i, (source, target) in enumerate(zip(small, rest))
    ]
    for load_ in first_loads + loads:
        load_.start()
    for load_ in first_loads:
        load_.wait()
    for i, matrix in enumerate(slot_matrices(own_scenarios(scen_ref, direct), False)):
        rows_ref[i] = matrix
    rows = see_ref.shape[0]
    ends, total = [], 0
    for i in range(lengths_ref.shape[1]):
        total = total + lengths_ref[0, i]
        ends.append(total)
    limits = [offsets_ref[0, i] for i in range(offsets_ref.shape[1])]
    first = lax.axis_index("seq") * rows
    shift = MB.bit_length() - 1

    def visible(query, key):
        query_hist, key_hist = history_of(query, ends), history_of(key, ends)
        near = (query >> shift) - (key >> shift) <= limit_of(query_hist, limits)
        return jnp.where((query_hist == key_hist) & (key <= query) & (key >= 0) & near, 1.0, 0.0)

    down = lax.broadcasted_iota(jnp.int32, (rows, rows), 0)
    along = lax.broadcasted_iota(jnp.int32, (rows, rows), 1)
    for block in range(blocks):
        span = slice(block * rows, (block + 1) * rows)
        see_ref[:, span] = visible(first + down, first - block * rows + along)
        seen_ref[:, span] = visible(first + block * rows + along, first + down)
    for load_ in loads:
        load_.wait()


def project_kernel(count, parts, w_ref, *refs):
    ins, outs, slope_ref = refs[:count], refs[count:-1], refs[-1]
    rows = unfold(ins)
    width = HEADS * HD
    done = []
    for i, part in enumerate(parts):
        pre = dot(rows, w_ref[:, part * width : (part + 1) * width])
        sig = sigmoid(pre)
        slope_ref[:, i * width : (i + 1) * width] = sig * (1.0 + pre * (1.0 - sig))
        done.append((pre * sig).astype(bf16))
    fold(jnp.concatenate(done, axis=1), outs)


def rows_kernel(rows_ref, *refs):
    matrices = [rows_ref[i] for i in range(1 + FOLD)]
    refs[-1][...] = from_slots(matrices, refs[:-1]).astype(bf16)


def head_cols(head, part=0):
    start = (part * HEADS + head) * HD
    return slice(start, start + HD)


def forward_kernel(blocks, see_ref, gq_ref, cotan_ref, *refs):
    pairs, (out_ref, grad_ref, gate_ref, mixed_ref) = refs[:blocks], refs[blocks:]
    rows = gq_ref.shape[0]
    scale = HD ** (-0.5)
    total = jnp.zeros((rows, 1), f32)
    for head in range(HEADS):
        query = gq_ref[:, head_cols(head, 1)]
        mixed = jnp.zeros((rows, HD), f32)
        for block in range(blocks):
            score = dot_nt(query, pairs[block][:, head_cols(head, 1)]) * scale
            weight = score * sigmoid(score) * see_ref[:, block * rows : (block + 1) * rows]
            mixed = mixed + dot(weight.astype(bf16), pairs[block][:, head_cols(head)])
        mixed_ref[:, head_cols(head)] = mixed
        total = total + jnp.sum(mixed * mixed, axis=1, keepdims=True)
    width = HEADS * HD
    row_scale = lax.rsqrt(total / width + eps)
    normed = mixed_ref[...] * row_scale
    gate = gq_ref[:, :width].astype(f32)
    cotan = cotan_ref[...].astype(f32)
    grad_norm = cotan * gate
    mean = jnp.mean(grad_norm * normed, axis=1, keepdims=True)
    grad_ref[...] = (row_scale * (grad_norm - normed * mean)).astype(bf16)
    out_ref[...] = (gate * normed).astype(bf16)
    gate_ref[...] = (cotan * normed).astype(bf16)


def slope_of(score):
    sig = sigmoid(score)
    return sig, sig * (1.0 + score * (1.0 - sig))


def wires_out(count, refs):
    return [refs[i : i + count] for i in range(0, len(refs), count)]


def query_kernel(count, blocks, see_ref, gq_ref, grad_ref, gate_ref, slots_ref, *refs):
    pairs, wires = refs[:blocks], wires_out(count, refs[blocks:])
    rows = gq_ref.shape[0]
    scale = HD ** (-0.5)
    done = []
    for head in range(HEADS):
        query = gq_ref[:, head_cols(head, 1)]
        grad = grad_ref[:, head_cols(head)]
        grad_query = jnp.zeros((rows, HD), f32)
        for block in range(blocks):
            key = pairs[block][:, head_cols(head, 1)]
            score = dot_nt(query, key) * scale
            _, slope = slope_of(score)
            att = dot_nt(grad, pairs[block][:, head_cols(head)])
            grad_score = att * slope * see_ref[:, block * rows : (block + 1) * rows]
            grad_query = grad_query + dot(grad_score.astype(bf16), key)
        done.append((grad_query * scale).astype(bf16))
    parts_to_slots(slots_ref, [gate_ref[...], jnp.concatenate(done, axis=1)], wires)


def key_kernel(count, blocks, seen_ref, pair_ref, slots_ref, *refs):
    queries, grads = refs[:blocks], refs[blocks : 2 * blocks]
    wires = wires_out(count, refs[2 * blocks :])
    rows = pair_ref.shape[0]
    scale = HD ** (-0.5)
    grad_keys, grad_values = [], []
    for head in range(HEADS):
        key = pair_ref[:, head_cols(head, 1)]
        value = pair_ref[:, head_cols(head)]
        grad_key = jnp.zeros((rows, HD), f32)
        grad_value = jnp.zeros((rows, HD), f32)
        for block in range(blocks):
            mask = seen_ref[:, block * rows : (block + 1) * rows]
            query = queries[block][:, head_cols(head, 1 if block == 0 else 0)]
            grad = grads[block][:, head_cols(head)]
            score = dot_nt(key, query) * scale
            sig, slope = slope_of(score)
            weight = score * sig * mask
            grad_score = dot_nt(value, grad) * slope * mask
            grad_key = grad_key + dot(grad_score.astype(bf16), query)
            grad_value = grad_value + dot(weight.astype(bf16), grad)
        grad_keys.append((grad_key * scale).astype(bf16))
        grad_values.append(grad_value.astype(bf16))
    parts = [jnp.concatenate(one, axis=1) for one in (grad_values, grad_keys)]
    parts_to_slots(slots_ref, parts, wires)


def owner_term(parts, refs, slope_ref, w_ref):
    width = HEADS * HD
    grad_pre = (unfold(refs).astype(f32) * slope_ref[...]).astype(bf16)
    term = None
    for i, part in enumerate(parts):
        one = dot_nt(
            grad_pre[:, i * width : (i + 1) * width], w_ref[:, part * width : (part + 1) * width]
        )
        term = one if term is None else term + one
    return term


def term_kernel(parts, slope_ref, w_ref, *refs):
    refs[-1][...] = owner_term(parts, refs[:-1], slope_ref, w_ref)


def last_term_kernel(count, parts, slope_ref, w_ref, *refs):
    ins, others, outs = refs[:count], refs[count:-count], refs[-count:]
    term = owner_term(parts, ins, slope_ref, w_ref)
    for other_ref in others:
        term = term + other_ref[...]
    fold(term.astype(bf16), outs)


def leave_kernel(count, rows_ref, events_ref, gain_ref, *refs):
    matrices = [rows_ref[i] for i in range(1 + FOLD)]
    wires = wires_out(count, refs[:-1])
    scaled = sum(from_slots(matrices, wire) for wire in wires) * gain_of(gain_ref)
    events = events_ref[...].astype(f32)
    row_inv = lax.rsqrt(jnp.mean(events * events, axis=1, keepdims=True) + eps)
    normed = events * row_inv
    mean = jnp.mean(scaled * normed, axis=1, keepdims=True)
    refs[-1][...] = (row_inv * (scaled - normed * mean)).astype(bf16)


def exchange(blocks):
    done = exchanged(blocks)
    if 1 < len(blocks) < lax.axis_size("user"):
        others = jnp.concatenate([block[MAIN:] for block in done], axis=0)
        done += [lax.ppermute(others, "user", [(i, i ^ 1) for i in range(lax.axis_size("user"))])]
    return done


def exchanged(blocks):
    count = lax.axis_size("user")
    if len(blocks) == 1:
        wire = blocks[0].reshape(-1, MAIN, blocks[0].shape[1])
        done = lax.all_to_all(wire, "user", split_axis=0, concat_axis=0, tiled=True)
        return [done.reshape(blocks[0].shape)]
    done = list(blocks)
    merged = count // len(blocks)
    for k in range(len(blocks) - 1, 0, -1):
        done[k] = lax.ppermute(blocks[k], "user", [(i, i ^ (merged * k)) for i in range(count)])
    return done


def shifted(block, distance):
    devices = range(lax.axis_size("seq"))
    route = [(i - distance, i) for i in devices if i - distance in devices]
    return lax.ppermute(block, "seq", route)


def wires_of(boxes):
    cols = boxes[0].shape[1]
    return [jnp.stack([box.reshape(SCEN, MAIN, cols) for box in boxes], axis=1).reshape(-1, cols)]


def slices_of(split, box):
    cols = box.shape[1]
    blocks = box.reshape(SCEN, split, MAIN, cols)
    return [blocks[:, i].reshape(-1, cols) for i in range(split)]


def shards(events, scenario, lengths, offsets, gain, w_proj, cotangent):
    n_seq = lax.axis_size("seq")
    n_user = lax.axis_size("user")
    split = n_user // SCEN
    rows, feats = events.shape[1:]
    width = HEADS * HD
    longest = n_seq * rows // 2
    reach = min(REACH, n_seq - 1, (longest - 2) // rows + 1)
    blocks = reach + 1
    direct = split == 1
    senders = SCEN if direct else 1

    def wire(rows, cols, merged=1):
        count = rows // (MAIN * merged) if direct else 1
        return [shape((rows // count, cols * (FOLD + 1) // FOLD), bf16)] * count

    slots = wire(SCEN * MAIN, feats)
    matrices = shape((1 + FOLD, rows, SCEN * MAIN), bf16)
    events, w_hbm, cotan = events[0], w_proj[0], cotangent[0]
    gain = gain.reshape(-1, LANES)

    to_slot, *outbox = call(
        functools.partial(enter_kernel, direct),
        [matrices] + slots,
        [events, gain, scenario],
        [pltpu.HBM] * 3,
        [
            pltpu.VMEM(events.shape, bf16),
            pltpu.VMEM(gain.shape, f32),
            pltpu.VMEM(scenario.shape, jnp.int32),
            pltpu.SemaphoreType.DMA((3,)),
        ],
        limit=VMEM_ALL - (1 << 20),
    )
    inbound = exchange(outbox if direct else wires_of(outbox * split))
    w_local, to_row, see, seen = call(
        functools.partial(mask_kernel, direct, blocks),
        [shape(w_hbm.shape, bf16), matrices] + [shape((rows, blocks * rows), f32)] * 2,
        [w_hbm, lengths, offsets, scenario],
        [pltpu.HBM] * 4,
        [
            pltpu.SMEM(lengths.shape, jnp.int32),
            pltpu.SMEM(offsets.shape, jnp.int32),
            pltpu.VMEM(scenario.shape, jnp.int32),
            pltpu.SemaphoreType.DMA((7,)),
        ],
    )

    def project(parts, merged=1):
        cols = len(parts) * width
        *box, slope = call(
            functools.partial(project_kernel, senders, parts),
            wire(n_user * MAIN, cols, merged) + [shape((n_user * CAP, cols), f32)],
            [w_local] + inbound,
        )
        return exchange(box), slope

    def rows_of(box):
        cols = box[0].shape[1] * FOLD // (FOLD + 1)
        return call(rows_kernel, [shape((rows, cols), bf16)], [to_row] + box)[0]

    if direct:
        pair_parts, query_parts = (1, 3), (0, 2)
        pair_back, pair_slope = project(pair_parts)
        query_back, query_slope = project(query_parts)
        pair_own = rows_of(pair_back)
        gq = rows_of(query_back)
    else:
        (box,), slope = project((0,))
        gate, value, query, key = [rows_of([part]) for part in slices_of(split, box)]
        pair_own = jnp.concatenate([value, key], axis=1)
        gq = jnp.concatenate([gate, query], axis=1)
    pairs = [pair_own] + [shifted(pair_own, d) for d in range(1, blocks)]
    query_own = gq[:, width:]
    queries = [gq] + [shifted(query_own, -d) for d in range(1, blocks)]
    half = shape((rows, width), bf16)
    output, grad_own, grad_gate, _ = call(
        functools.partial(forward_kernel, blocks),
        [half, half, half, shape((rows, width), f32)],
        [see, gq, cotan] + pairs,
    )
    grads = [grad_own] + [shifted(grad_own, -d) for d in range(1, blocks)]

    def boxes(merged=1):
        cols = 2 * width if direct else width
        return wire(SCEN * MAIN, cols, merged) * (1 if direct else 2)

    query_grad = call(
        functools.partial(query_kernel, len(boxes(2)) if direct else 1, blocks),
        boxes(2),
        [see, gq, grad_own, grad_gate, to_slot] + pairs,
    )
    pair_grad = call(
        functools.partial(key_kernel, senders, blocks),
        boxes(),
        [seen, pair_own, to_slot] + queries + grads,
    )
    term = shape((n_user * CAP, feats), f32)
    if direct:
        (query_term,) = call(
            functools.partial(term_kernel, query_parts),
            [term],
            [query_slope, w_local] + exchange(query_grad),
        )
        last_parts, last = pair_parts, [pair_slope, w_local] + exchange(pair_grad) + [query_term]
    else:
        order = [query_grad[0], pair_grad[0], query_grad[1], pair_grad[1]]
        last_parts, last = (0,), [slope, w_local] + exchange(wires_of(order))
    term_box = call(
        functools.partial(last_term_kernel, senders, last_parts), wire(n_user * MAIN, feats), last
    )
    term_back = exchange(term_box)
    (grad_events,) = call(
        functools.partial(leave_kernel, senders),
        [shape((rows, feats), bf16)],
        [to_row, events, gain] + (term_back if direct else slices_of(split, term_back[0])),
    )
    return output[None], grad_events[None]


def solution(mesh):
    placed = (
        P("user", "seq", None),
        P("user", "seq"),
        P("user", None),
        P("user", None),
        P(),
        P("user", None, None),
        P("user", "seq", None),
    )
    return jax.shard_map(
        shards,
        mesh=mesh,
        in_specs=placed,
        out_specs=(P("user", "seq", None), P("user", "seq", None)),
        check_vma=False,
    )
```

```python
import functools

import jax
import jax.numpy as jnp
from jax import lax
from jax.experimental import pallas as pl
from jax.experimental.pallas import tpu as pltpu
from jax.sharding import PartitionSpec as P


HEADS = 6
HD = 128
SCEN = 8
MB = 128
CAP = 20
REACH = 4

MAIN = 16
EXTRA = CAP - MAIN
FOLD = MAIN // EXTRA

VMEM_LIMIT = 24 << 20
VMEM_ALL = 67043328
LANES = 128

eps = 1e-05
f32 = jnp.float32
bf16 = jnp.bfloat16
NT = (((1,), (1,)), ((), ()))


def call(kernel, outs, operands, spaces=(), scratch=(), flops=1 << 24, limit=VMEM_LIMIT):
    spaces = list(spaces) + [pltpu.VMEM] * (len(operands) - len(spaces))
    moved = sum(o.size * o.dtype.itemsize for o in list(outs) + list(operands))
    return pl.pallas_call(
        kernel,
        out_shape=tuple(outs),
        in_specs=[pl.BlockSpec(memory_space=space) for space in spaces],
        out_specs=tuple(pl.BlockSpec(memory_space=pltpu.VMEM) for _ in outs),
        scratch_shapes=list(scratch),
        cost_estimate=pl.CostEstimate(flops=flops, bytes_accessed=moved, transcendentals=0),
        compiler_params=pltpu.CompilerParams(vmem_limit_bytes=limit),
    )(*operands)


def shape(dims, dtype):
    return jax.ShapeDtypeStruct(dims, dtype)


def dot(a, b):
    return jnp.dot(a, b, preferred_element_type=f32)


def dot_nt(a, b):
    return lax.dot_general(a, b, NT, preferred_element_type=f32)


def sigmoid(v):
    return 0.5 * jnp.tanh(0.5 * v) + 0.5


def iotas(rows, cols):
    return (
        lax.broadcasted_iota(jnp.int32, (rows, cols), 0),
        lax.broadcasted_iota(jnp.int32, (rows, cols), 1),
    )


def hot(condition):
    return jnp.where(condition, 1.0, 0.0).astype(bf16)


def load(refs, cols):
    if swapped(refs):
        parts = []
        for i, ref in enumerate(refs[:-1]):
            parts += [ref[:MAIN, cols], refs[-1][i * MAIN : (i + 1) * MAIN, cols]]
    else:
        parts = [ref[:, cols] for ref in refs]
    return parts[0] if len(parts) == 1 else jnp.concatenate(parts, axis=0)


def swapped(refs):
    return len(refs) > 1 and refs[0].shape[0] == 2 * MAIN


def rows_in(refs):
    return 2 * refs[-1].shape[0] if swapped(refs) else sum(ref.shape[0] for ref in refs)


def store(refs, cols, value):
    rows = refs[0].shape[0]
    for i, ref in enumerate(refs):
        ref[:, cols] = value[i * rows : (i + 1) * rows]


def main_cols(refs):
    return refs[0].shape[1] * FOLD // (FOLD + 1)


def slot_matrices(scen_row, by_slot):
    rows = scen_row.shape[1]
    down, along = iotas(rows, rows)
    scen_b = jnp.broadcast_to(scen_row.astype(f32), (rows, rows))
    scen_col = jnp.sum(jnp.where(down == along, scen_b, 0.0), axis=1, keepdims=True)
    same = scen_b == scen_col
    if by_slot:
        scen = scen_row.astype(f32)
        rank = jnp.sum(jnp.where(same & (down < along), 1.0, 0.0), axis=0, keepdims=True)
        down, along = iotas(SCEN * MAIN, rows)
        slot = down.astype(f32)
    else:
        scen = scen_col
        rank = jnp.sum(jnp.where(same & (along < down), 1.0, 0.0), axis=1, keepdims=True)
        down, along = iotas(rows, SCEN * MAIN)
        slot = along.astype(f32)
    main = jnp.where(rank < MAIN, scen * MAIN + rank, -1.0)
    out = [hot(slot == main)]
    for piece in range(FOLD):
        extra = jnp.where(rank >= MAIN, scen * MAIN + EXTRA * piece + (rank - MAIN), -1.0)
        out.append(hot(slot == extra))
    return out


def to_slots(matrices, value, refs):
    cols = value.shape[1]
    piece = cols // FOLD
    store(refs, slice(0, cols), dot(matrices[0], value).astype(bf16))
    extra = dot(matrices[1], value[:, :piece])
    for part in range(1, FOLD):
        extra = extra + dot(matrices[1 + part], value[:, part * piece : (part + 1) * piece])
    store(refs, slice(cols, cols + piece), extra.astype(bf16))


def from_slots(matrices, refs):
    cols = main_cols(refs)
    piece = cols // FOLD
    extra = load(refs, slice(cols, cols + piece))
    out = []
    for part in range(FOLD):
        left = jnp.concatenate([matrices[0], matrices[1 + part]], axis=1)
        right = jnp.concatenate([load(refs, slice(part * piece, (part + 1) * piece)), extra], axis=0)
        out.append(dot(left, right))
    return jnp.concatenate(out, axis=1)


def parts_to_slots(slots_ref, parts, wires):
    matrices = [slots_ref[i] for i in range(1 + FOLD)]
    if len(wires) == 1:
        parts = [jnp.concatenate(parts, axis=1)]
    for part, refs in zip(parts, wires):
        to_slots(matrices, part, refs)


def extra_matrix(count, part, by_row):
    if by_row:
        down, along = iotas(count * EXTRA, count * MAIN)
    else:
        along, down = iotas(count * MAIN, count * EXTRA)
    group = sum((down >= EXTRA * i).astype(jnp.int32) for i in range(1, count))
    return hot(along == down + group * (MAIN - EXTRA) + EXTRA * part)


def unfold(refs):
    count = rows_in(refs) // MAIN
    cols = main_cols(refs)
    extra = load(refs, slice(cols, cols + cols // FOLD))
    pieces = [dot(extra_matrix(count, part, True), extra) for part in range(FOLD)]
    extra = jnp.concatenate(pieces, axis=1).astype(bf16)
    return jnp.concatenate([load(refs, slice(0, cols)), extra], axis=0)


def fold(value, refs):
    rows, cols = sum(ref.shape[0] for ref in refs), value.shape[1]
    count = rows // MAIN
    piece = cols // FOLD
    store(refs, slice(0, cols), value[:rows])
    extra = sum(
        dot(extra_matrix(count, part, False), value[rows:, part * piece : (part + 1) * piece])
        for part in range(FOLD)
    )
    store(refs, slice(cols, cols + piece), extra.astype(bf16))


def own_scenarios(scen_ref, direct):
    return scen_ref[...] ^ lax.axis_index("user") if direct else scen_ref[...]


def gain_of(gain_ref):
    return jnp.concatenate([gain_ref[i : i + 1] for i in range(gain_ref.shape[0])], axis=1)


def enter_kernel(direct, events_hbm, gain_hbm, scen_hbm, slots_ref, *refs):
    events_ref, gain_ref, scen_ref, sems = refs[-4:]
    refs = refs[:-4]
    loads = [
        pltpu.make_async_copy(source, target, sems.at[i])
        for i, (source, target) in enumerate(
            [(events_hbm, events_ref), (gain_hbm, gain_ref), (scen_hbm, scen_ref)]
        )
    ]
    for load_ in loads:
        load_.start()
    for load_ in loads:
        load_.wait()
    events = events_ref[...].astype(f32)
    row_inv = lax.rsqrt(jnp.mean(events * events, axis=1, keepdims=True) + eps)
    normed = (events * row_inv * gain_of(gain_ref)).astype(bf16)
    matrices = slot_matrices(own_scenarios(scen_ref, direct), True)
    for i, matrix in enumerate(matrices):
        slots_ref[i] = matrix
    to_slots(matrices, normed, refs)


def history_of(pos, ends):
    return sum((pos >= end).astype(jnp.int32) for end in ends)


def limit_of(history, limits):
    return sum(jnp.where(history == i, limit, 0) for i, limit in enumerate(limits))


def mask_kernel(direct, blocks, w_hbm, *refs):
    small, (w_ref, rows_ref, see_ref, seen_ref), rest = refs[:3], refs[3:7], refs[7:]
    lengths_ref, offsets_ref, scen_ref, sems = rest
    count = sems.shape[0] - len(small)
    depth = w_ref.shape[0] // count
    loads = [
        pltpu.make_async_copy(
            w_hbm.at[pl.ds(i * depth, depth)], w_ref.at[pl.ds(i * depth, depth)], sems.at[i]
        )
        for i in range(count)
    ]
    first_loads = [
        pltpu.make_async_copy(source, target, sems.at[count + i])
        for i, (source, target) in enumerate(zip(small, rest))
    ]
    for load_ in first_loads + loads:
        load_.start()
    for load_ in first_loads:
        load_.wait()
    for i, matrix in enumerate(slot_matrices(own_scenarios(scen_ref, direct), False)):
        rows_ref[i] = matrix
    rows = see_ref.shape[0]
    ends, total = [], 0
    for i in range(lengths_ref.shape[1]):
        total = total + lengths_ref[0, i]
        ends.append(total)
    limits = [offsets_ref[0, i] for i in range(offsets_ref.shape[1])]
    first = lax.axis_index("seq") * rows
    shift = MB.bit_length() - 1

    def visible(query, key):
        query_hist, key_hist = history_of(query, ends), history_of(key, ends)
        near = (query >> shift) - (key >> shift) <= limit_of(query_hist, limits)
        return jnp.where((query_hist == key_hist) & (key <= query) & (key >= 0) & near, 1.0, 0.0)

    down = lax.broadcasted_iota(jnp.int32, (rows, rows), 0)
    along = lax.broadcasted_iota(jnp.int32, (rows, rows), 1)
    for block in range(blocks):
        span = slice(block * rows, (block + 1) * rows)
        see_ref[:, span] = visible(first + down, first - block * rows + along)
        seen_ref[:, span] = visible(first + block * rows + along, first + down)
    for load_ in loads:
        load_.wait()


def project_kernel(count, parts, w_ref, *refs):
    ins, outs, slope_ref = refs[:count], refs[count:-1], refs[-1]
    rows = unfold(ins)
    width = HEADS * HD
    done = []
    for i, part in enumerate(parts):
        pre = dot(rows, w_ref[:, part * width : (part + 1) * width])
        sig = sigmoid(pre)
        slope_ref[:, i * width : (i + 1) * width] = sig * (1.0 + pre * (1.0 - sig))
        done.append((pre * sig).astype(bf16))
    fold(jnp.concatenate(done, axis=1), outs)


def rows_kernel(rows_ref, *refs):
    matrices = [rows_ref[i] for i in range(1 + FOLD)]
    refs[-1][...] = from_slots(matrices, refs[:-1]).astype(bf16)


def head_cols(head, part=0):
    start = (part * HEADS + head) * HD
    return slice(start, start + HD)


def forward_kernel(blocks, see_ref, gq_ref, cotan_ref, *refs):
    pairs, (out_ref, grad_ref, gate_ref, mixed_ref) = refs[:blocks], refs[blocks:]
    rows = gq_ref.shape[0]
    scale = HD ** (-0.5)
    total = jnp.zeros((rows, 1), f32)
    for head in range(HEADS):
        query = gq_ref[:, head_cols(head, 1)]
        mixed = jnp.zeros((rows, HD), f32)
        for block in range(blocks):
            score = dot_nt(query, pairs[block][:, head_cols(head, 1)]) * scale
            weight = score * sigmoid(score) * see_ref[:, block * rows : (block + 1) * rows]
            mixed = mixed + dot(weight.astype(bf16), pairs[block][:, head_cols(head)])
        mixed_ref[:, head_cols(head)] = mixed
        total = total + jnp.sum(mixed * mixed, axis=1, keepdims=True)
    width = HEADS * HD
    row_scale = lax.rsqrt(total / width + eps)
    normed = mixed_ref[...] * row_scale
    gate = gq_ref[:, :width].astype(f32)
    cotan = cotan_ref[...].astype(f32)
    grad_norm = cotan * gate
    mean = jnp.mean(grad_norm * normed, axis=1, keepdims=True)
    grad_ref[...] = (row_scale * (grad_norm - normed * mean)).astype(bf16)
    out_ref[...] = (gate * normed).astype(bf16)
    gate_ref[...] = (cotan * normed).astype(bf16)


def slope_of(score):
    sig = sigmoid(score)
    return sig, sig * (1.0 + score * (1.0 - sig))


def wires_out(count, refs):
    return [refs[i : i + count] for i in range(0, len(refs), count)]


def query_kernel(count, blocks, see_ref, gq_ref, grad_ref, gate_ref, slots_ref, *refs):
    pairs, wires = refs[:blocks], wires_out(count, refs[blocks:])
    rows = gq_ref.shape[0]
    scale = HD ** (-0.5)
    done = []
    for head in range(HEADS):
        query = gq_ref[:, head_cols(head, 1)]
        grad = grad_ref[:, head_cols(head)]
        grad_query = jnp.zeros((rows, HD), f32)
        for block in range(blocks):
            key = pairs[block][:, head_cols(head, 1)]
            score = dot_nt(query, key) * scale
            _, slope = slope_of(score)
            att = dot_nt(grad, pairs[block][:, head_cols(head)])
            grad_score = att * slope * see_ref[:, block * rows : (block + 1) * rows]
            grad_query = grad_query + dot(grad_score.astype(bf16), key)
        done.append((grad_query * scale).astype(bf16))
    parts_to_slots(slots_ref, [gate_ref[...], jnp.concatenate(done, axis=1)], wires)


def key_kernel(count, blocks, seen_ref, pair_ref, slots_ref, *refs):
    queries, grads = refs[:blocks], refs[blocks : 2 * blocks]
    wires = wires_out(count, refs[2 * blocks :])
    rows = pair_ref.shape[0]
    scale = HD ** (-0.5)
    grad_keys, grad_values = [], []
    for head in range(HEADS):
        key = pair_ref[:, head_cols(head, 1)]
        value = pair_ref[:, head_cols(head)]
        grad_key = jnp.zeros((rows, HD), f32)
        grad_value = jnp.zeros((rows, HD), f32)
        for block in range(blocks):
            mask = seen_ref[:, block * rows : (block + 1) * rows]
            query = queries[block][:, head_cols(head, 1 if block == 0 else 0)]
            grad = grads[block][:, head_cols(head)]
            score = dot_nt(key, query) * scale
            sig, slope = slope_of(score)
            weight = score * sig * mask
            grad_score = dot_nt(value, grad) * slope * mask
            grad_key = grad_key + dot(grad_score.astype(bf16), query)
            grad_value = grad_value + dot(weight.astype(bf16), grad)
        grad_keys.append((grad_key * scale).astype(bf16))
        grad_values.append(grad_value.astype(bf16))
    parts = [jnp.concatenate(one, axis=1) for one in (grad_values, grad_keys)]
    parts_to_slots(slots_ref, parts, wires)


def owner_term(parts, refs, slope_ref, w_ref):
    width = HEADS * HD
    grad_pre = (unfold(refs).astype(f32) * slope_ref[...]).astype(bf16)
    term = None
    for i, part in enumerate(parts):
        one = dot_nt(
            grad_pre[:, i * width : (i + 1) * width], w_ref[:, part * width : (part + 1) * width]
        )
        term = one if term is None else term + one
    return term


def term_kernel(parts, slope_ref, w_ref, *refs):
    refs[-1][...] = owner_term(parts, refs[:-1], slope_ref, w_ref)


def last_term_kernel(count, parts, slope_ref, w_ref, *refs):
    ins, others, outs = refs[:count], refs[count:-count], refs[-count:]
    term = owner_term(parts, ins, slope_ref, w_ref)
    for other_ref in others:
        term = term + other_ref[...]
    fold(term.astype(bf16), outs)


def leave_kernel(count, rows_ref, events_ref, gain_ref, *refs):
    matrices = [rows_ref[i] for i in range(1 + FOLD)]
    wires = wires_out(count, refs[:-1])
    scaled = sum(from_slots(matrices, wire) for wire in wires) * gain_of(gain_ref)
    events = events_ref[...].astype(f32)
    row_inv = lax.rsqrt(jnp.mean(events * events, axis=1, keepdims=True) + eps)
    normed = events * row_inv
    mean = jnp.mean(scaled * normed, axis=1, keepdims=True)
    refs[-1][...] = (row_inv * (scaled - normed * mean)).astype(bf16)


def exchange(blocks):
    done = exchanged(blocks)
    if 1 < len(blocks) < lax.axis_size("user"):
        others = jnp.concatenate([block[MAIN:] for block in done], axis=0)
        done += [lax.ppermute(others, "user", [(i, i ^ 1) for i in range(lax.axis_size("user"))])]
    return done


def exchanged(blocks):
    count = lax.axis_size("user")
    if len(blocks) == 1:
        wire = blocks[0].reshape(-1, MAIN, blocks[0].shape[1])
        done = lax.all_to_all(wire, "user", split_axis=0, concat_axis=0, tiled=True)
        return [done.reshape(blocks[0].shape)]
    done = list(blocks)
    merged = count // len(blocks)
    for k in range(1, len(blocks)):
        done[k] = lax.ppermute(blocks[k], "user", [(i, i ^ (merged * k)) for i in range(count)])
    return done


def shifted(block, distance):
    count = lax.axis_size("seq")
    route = [((i - distance) % count, i) for i in range(count)]
    return lax.ppermute(block, "seq", route)


def wires_of(boxes):
    cols = boxes[0].shape[1]
    return [jnp.stack([box.reshape(SCEN, MAIN, cols) for box in boxes], axis=1).reshape(-1, cols)]


def slices_of(split, box):
    cols = box.shape[1]
    blocks = box.reshape(SCEN, split, MAIN, cols)
    return [blocks[:, i].reshape(-1, cols) for i in range(split)]


def shards(events, scenario, lengths, offsets, gain, w_proj, cotangent):
    n_seq = lax.axis_size("seq")
    n_user = lax.axis_size("user")
    split = n_user // SCEN
    rows, feats = events.shape[1:]
    width = HEADS * HD
    longest = n_seq * rows // 2
    reach = min(REACH, n_seq - 1, (longest - 2) // rows + 1)
    blocks = reach + 1
    direct = split == 1
    senders = SCEN if direct else 1

    def wire(rows, cols, merged=1):
        count = rows // (MAIN * merged) if direct else 1
        return [shape((rows // count, cols * (FOLD + 1) // FOLD), bf16)] * count

    slots = wire(SCEN * MAIN, feats)
    matrices = shape((1 + FOLD, rows, SCEN * MAIN), bf16)
    events, w_hbm, cotan = events[0], w_proj[0], cotangent[0]
    gain = gain.reshape(-1, LANES)

    to_slot, *outbox = call(
        functools.partial(enter_kernel, direct),
        [matrices] + slots,
        [events, gain, scenario],
        [pltpu.HBM] * 3,
        [
            pltpu.VMEM(events.shape, bf16),
            pltpu.VMEM(gain.shape, f32),
            pltpu.VMEM(scenario.shape, jnp.int32),
            pltpu.SemaphoreType.DMA((3,)),
        ],
        limit=VMEM_ALL - (1 << 20),
    )
    inbound = exchange(outbox if direct else wires_of(outbox * split))
    w_local, to_row, see, seen = call(
        functools.partial(mask_kernel, direct, blocks),
        [shape(w_hbm.shape, bf16), matrices] + [shape((rows, blocks * rows), f32)] * 2,
        [w_hbm, lengths, offsets, scenario],
        [pltpu.HBM] * 4,
        [
            pltpu.SMEM(lengths.shape, jnp.int32),
            pltpu.SMEM(offsets.shape, jnp.int32),
            pltpu.VMEM(scenario.shape, jnp.int32),
            pltpu.SemaphoreType.DMA((7,)),
        ],
    )

    def project(parts, merged=1):
        cols = len(parts) * width
        *box, slope = call(
            functools.partial(project_kernel, senders, parts),
            wire(n_user * MAIN, cols, merged) + [shape((n_user * CAP, cols), f32)],
            [w_local] + inbound,
        )
        return exchange(box), slope

    def rows_of(box):
        cols = box[0].shape[1] * FOLD // (FOLD + 1)
        return call(rows_kernel, [shape((rows, cols), bf16)], [to_row] + box)[0]

    if direct:
        pair_parts, query_parts = (1, 3), (0, 2)
        pair_back, pair_slope = project(pair_parts)
        query_back, query_slope = project(query_parts)
        pair_own = rows_of(pair_back)
        gq = rows_of(query_back)
    else:
        (box,), slope = project((0,))
        gate, value, query, key = [rows_of([part]) for part in slices_of(split, box)]
        pair_own = jnp.concatenate([value, key], axis=1)
        gq = jnp.concatenate([gate, query], axis=1)
    pairs = [pair_own] + [shifted(pair_own, d) for d in range(1, blocks)]
    query_own = gq[:, width:]
    queries = [gq] + [shifted(query_own, -d) for d in range(1, blocks)]
    half = shape((rows, width), bf16)
    output, grad_own, grad_gate, _ = call(
        functools.partial(forward_kernel, blocks),
        [half, half, half, shape((rows, width), f32)],
        [see, gq, cotan] + pairs,
    )
    grads = [grad_own] + [shifted(grad_own, -d) for d in range(1, blocks)]

    def boxes(merged=1):
        cols = 2 * width if direct else width
        return wire(SCEN * MAIN, cols, merged) * (1 if direct else 2)

    query_grad = call(
        functools.partial(query_kernel, len(boxes(2)) if direct else 1, blocks),
        boxes(2),
        [see, gq, grad_own, grad_gate, to_slot] + pairs,
    )
    pair_grad = call(
        functools.partial(key_kernel, senders, blocks),
        boxes(),
        [seen, pair_own, to_slot] + queries + grads,
    )
    term = shape((n_user * CAP, feats), f32)
    if direct:
        (query_term,) = call(
            functools.partial(term_kernel, query_parts),
            [term],
            [query_slope, w_local] + exchange(query_grad),
        )
        last_parts, last = pair_parts, [pair_slope, w_local] + exchange(pair_grad) + [query_term]
    else:
        order = [query_grad[0], pair_grad[0], query_grad[1], pair_grad[1]]
        last_parts, last = (0,), [slope, w_local] + exchange(wires_of(order))
    term_box = call(
        functools.partial(last_term_kernel, senders, last_parts), wire(n_user * MAIN, feats), last
    )
    term_back = exchange(term_box)
    (grad_events,) = call(
        functools.partial(leave_kernel, senders),
        [shape((rows, feats), bf16)],
        [to_row, events, gain] + (term_back if direct else slices_of(split, term_back[0])),
    )
    return output[None], grad_events[None]


def solution(mesh):
    placed = (
        P("user", "seq", None),
        P("user", "seq"),
        P("user", None),
        P("user", None),
        P(),
        P("user", None, None),
        P("user", "seq", None),
    )
    return jax.shard_map(
        shards,
        mesh=mesh,
        in_specs=placed,
        out_specs=(P("user", "seq", None), P("user", "seq", None)),
        check_vma=False,
    )
```

```python
import functools

import jax
import jax.numpy as jnp
from jax import lax
from jax.experimental import pallas as pl
from jax.experimental.pallas import tpu as pltpu
from jax.sharding import PartitionSpec as P


HEADS = 6
HD = 128
SCEN = 8
MB = 128
CAP = 20
REACH = 4

MAIN = 16
EXTRA = CAP - MAIN
FOLD = MAIN // EXTRA

VMEM_LIMIT = 24 << 20
LANES = 128

eps = 1e-05
f32 = jnp.float32
bf16 = jnp.bfloat16
NT = (((1,), (1,)), ((), ()))


def call(kernel, outs, operands, spaces=(), scratch=(), flops=1 << 24, limit=VMEM_LIMIT):
    spaces = list(spaces) + [pltpu.VMEM] * (len(operands) - len(spaces))
    moved = sum(o.size * o.dtype.itemsize for o in list(outs) + list(operands))
    operands = [
        pltpu.with_memory_space_constraint(operand, space) if space == pltpu.HBM else operand
        for operand, space in zip(operands, spaces)
    ]
    return pl.pallas_call(
        kernel,
        out_shape=tuple(outs),
        in_specs=[pl.BlockSpec(memory_space=space) for space in spaces],
        out_specs=tuple(pl.BlockSpec(memory_space=pltpu.VMEM) for _ in outs),
        scratch_shapes=list(scratch),
        cost_estimate=pl.CostEstimate(flops=flops, bytes_accessed=moved, transcendentals=0),
        compiler_params=pltpu.CompilerParams(vmem_limit_bytes=limit),
    )(*operands)


def shape(dims, dtype):
    return jax.ShapeDtypeStruct(dims, dtype)


def dot(a, b):
    return jnp.dot(a, b, preferred_element_type=f32)


def dot_nt(a, b):
    return lax.dot_general(a, b, NT, preferred_element_type=f32)


def sigmoid(v):
    return 0.5 * jnp.tanh(0.5 * v) + 0.5


def iotas(rows, cols):
    return (
        lax.broadcasted_iota(jnp.int32, (rows, cols), 0),
        lax.broadcasted_iota(jnp.int32, (rows, cols), 1),
    )


def hot(condition):
    return jnp.where(condition, 1.0, 0.0).astype(bf16)


def load(refs, cols):
    if swapped(refs):
        parts = []
        for i, ref in enumerate(refs[:-1]):
            parts += [ref[:MAIN, cols], refs[-1][i * MAIN : (i + 1) * MAIN, cols]]
    else:
        parts = [ref[:, cols] for ref in refs]
    return parts[0] if len(parts) == 1 else jnp.concatenate(parts, axis=0)


def swapped(refs):
    return len(refs) > 1 and refs[0].shape[0] == 2 * MAIN


def rows_in(refs):
    return 2 * refs[-1].shape[0] if swapped(refs) else sum(ref.shape[0] for ref in refs)


def store(refs, cols, value):
    rows = refs[0].shape[0]
    for i, ref in enumerate(refs):
        ref[:, cols] = value[i * rows : (i + 1) * rows]


def main_cols(refs):
    return refs[0].shape[1] * FOLD // (FOLD + 1)


def slot_matrices(scen_row, by_slot):
    rows = scen_row.shape[1]
    down, along = iotas(rows, rows)
    scen_b = jnp.broadcast_to(scen_row.astype(f32), (rows, rows))
    scen_col = jnp.sum(jnp.where(down == along, scen_b, 0.0), axis=1, keepdims=True)
    same = scen_b == scen_col
    if by_slot:
        scen = scen_row.astype(f32)
        rank = jnp.sum(jnp.where(same & (down < along), 1.0, 0.0), axis=0, keepdims=True)
        down, along = iotas(SCEN * MAIN, rows)
        slot = down.astype(f32)
    else:
        scen = scen_col
        rank = jnp.sum(jnp.where(same & (along < down), 1.0, 0.0), axis=1, keepdims=True)
        down, along = iotas(rows, SCEN * MAIN)
        slot = along.astype(f32)
    main = jnp.where(rank < MAIN, scen * MAIN + rank, -1.0)
    out = [hot(slot == main)]
    for piece in range(FOLD):
        extra = jnp.where(rank >= MAIN, scen * MAIN + EXTRA * piece + (rank - MAIN), -1.0)
        out.append(hot(slot == extra))
    return out


def to_slots(matrices, value, refs):
    cols = value.shape[1]
    piece = cols // FOLD
    store(refs, slice(0, cols), dot(matrices[0], value).astype(bf16))
    extra = dot(matrices[1], value[:, :piece])
    for part in range(1, FOLD):
        extra = extra + dot(matrices[1 + part], value[:, part * piece : (part + 1) * piece])
    store(refs, slice(cols, cols + piece), extra.astype(bf16))


def from_slots(matrices, refs):
    cols = main_cols(refs)
    piece = cols // FOLD
    extra = load(refs, slice(cols, cols + piece))
    out = []
    for part in range(FOLD):
        left = jnp.concatenate([matrices[0], matrices[1 + part]], axis=1)
        right = jnp.concatenate([load(refs, slice(part * piece, (part + 1) * piece)), extra], axis=0)
        out.append(dot(left, right))
    return jnp.concatenate(out, axis=1)


def parts_to_slots(slots_ref, parts, wires):
    matrices = [slots_ref[i] for i in range(1 + FOLD)]
    if len(wires) == 1:
        parts = [jnp.concatenate(parts, axis=1)]
    for part, refs in zip(parts, wires):
        to_slots(matrices, part, refs)


def extra_matrix(count, part, by_row):
    if by_row:
        down, along = iotas(count * EXTRA, count * MAIN)
    else:
        along, down = iotas(count * MAIN, count * EXTRA)
    group = sum((down >= EXTRA * i).astype(jnp.int32) for i in range(1, count))
    return hot(along == down + group * (MAIN - EXTRA) + EXTRA * part)


def unfold(refs):
    count = rows_in(refs) // MAIN
    cols = main_cols(refs)
    extra = load(refs, slice(cols, cols + cols // FOLD))
    pieces = [dot(extra_matrix(count, part, True), extra) for part in range(FOLD)]
    extra = jnp.concatenate(pieces, axis=1).astype(bf16)
    return jnp.concatenate([load(refs, slice(0, cols)), extra], axis=0)


def fold(value, refs):
    rows, cols = sum(ref.shape[0] for ref in refs), value.shape[1]
    count = rows // MAIN
    piece = cols // FOLD
    store(refs, slice(0, cols), value[:rows])
    extra = sum(
        dot(extra_matrix(count, part, False), value[rows:, part * piece : (part + 1) * piece])
        for part in range(FOLD)
    )
    store(refs, slice(cols, cols + piece), extra.astype(bf16))


def own_scenarios(scen_ref, direct):
    return scen_ref[...] ^ lax.axis_index("user") if direct else scen_ref[...]


def gain_of(gain_ref):
    return jnp.concatenate([gain_ref[i : i + 1] for i in range(gain_ref.shape[0])], axis=1)


def enter_kernel(direct, events_hbm, gain_hbm, scen_hbm, slots_ref, *refs):
    events_ref, gain_ref, scen_ref, sems = refs[-4:]
    refs = refs[:-4]
    loads = [
        pltpu.make_async_copy(source, target, sems.at[i])
        for i, (source, target) in enumerate(
            [(events_hbm, events_ref), (gain_hbm, gain_ref), (scen_hbm, scen_ref)]
        )
    ]
    for load_ in reversed(loads):
        load_.start()
    loads[2].wait()
    matrices = slot_matrices(own_scenarios(scen_ref, direct), True)
    for i, matrix in enumerate(matrices):
        slots_ref[i] = matrix
    loads[1].wait()
    loads[0].wait()
    events = events_ref[...].astype(f32)
    row_inv = lax.rsqrt(jnp.mean(events * events, axis=1, keepdims=True) + eps)
    normed = (events * row_inv * gain_of(gain_ref)).astype(bf16)
    to_slots(matrices, normed, refs)


def history_of(pos, ends):
    return sum((pos >= end).astype(jnp.int32) for end in ends)


def limit_of(history, limits):
    return sum(jnp.where(history == i, limit, 0) for i, limit in enumerate(limits))


def mask_kernel(
    direct, blocks, histories, w_hbm, small_ref, w_ref, rows_ref, see_ref, seen_ref, sems
):
    count = sems.shape[0]
    depth = w_ref.shape[0] // count
    loads = [
        pltpu.make_async_copy(
            w_hbm.at[pl.ds(i * depth, depth)], w_ref.at[pl.ds(i * depth, depth)], sems.at[i]
        )
        for i in range(count)
    ]
    for load_ in loads:
        load_.start()
    for i, matrix in enumerate(
        slot_matrices(own_scenarios(small_ref.at[:, 2 * histories :], direct), False)
    ):
        rows_ref[i] = matrix
    rows = see_ref.shape[0]
    ends, total = [], 0
    for i in range(histories):
        total = total + small_ref[:, i : i + 1]
        ends.append(total)
    limits = [small_ref[:, i : i + 1] for i in range(histories, 2 * histories)]
    first = lax.axis_index("seq") * rows
    shift = MB.bit_length() - 1

    def visible(query, key):
        query_hist, key_hist = history_of(query, ends), history_of(key, ends)
        near = (query >> shift) - (key >> shift) <= limit_of(query_hist, limits)
        return jnp.where((query_hist == key_hist) & (key <= query) & (key >= 0) & near, 1.0, 0.0)

    down = lax.broadcasted_iota(jnp.int32, (rows, rows), 0)
    along = lax.broadcasted_iota(jnp.int32, (rows, rows), 1)
    for block in range(blocks):
        span = slice(block * rows, (block + 1) * rows)
        see_ref[:, span] = visible(first + down, first - block * rows + along)
        seen_ref[:, span] = visible(first + block * rows + along, first + down)
    for load_ in loads:
        load_.wait()


def project_kernel(count, parts, w_ref, *refs):
    ins, outs, slope_ref = refs[:count], refs[count:-1], refs[-1]
    rows = unfold(ins)
    width = HEADS * HD
    done = []
    for i, part in enumerate(parts):
        pre = dot(rows, w_ref[:, part * width : (part + 1) * width])
        sig = sigmoid(pre)
        slope_ref[:, i * width : (i + 1) * width] = sig * (1.0 + pre * (1.0 - sig))
        done.append((pre * sig).astype(bf16))
    fold(jnp.concatenate(done, axis=1), outs)


def rows_kernel(rows_ref, *refs):
    matrices = [rows_ref[i] for i in range(1 + FOLD)]
    refs[-1][...] = from_slots(matrices, refs[:-1]).astype(bf16)


def head_cols(head, part=0):
    start = (part * HEADS + head) * HD
    return slice(start, start + HD)


def stack(refs, cols):
    return jnp.concatenate([ref[:, cols] for ref in refs], axis=0)


def forward_kernel(blocks, see_ref, gq_ref, cotan_ref, *refs):
    pairs, (out_ref, grad_ref, gate_ref) = refs[:blocks], refs[blocks:]
    scale = HD ** (-0.5)
    see = see_ref[...]
    done = []
    for head in range(HEADS):
        keys = stack(pairs, head_cols(head, 1))
        score = dot_nt(gq_ref[:, head_cols(head, 1)], keys) * scale
        weight = (score * sigmoid(score) * see).astype(bf16)
        done.append(dot(weight, stack(pairs, head_cols(head))))
    width = HEADS * HD
    mixed = jnp.concatenate(done, axis=1)
    row_scale = lax.rsqrt(jnp.mean(mixed * mixed, axis=1, keepdims=True) + eps)
    normed = mixed * row_scale
    gate = gq_ref[:, :width].astype(f32)
    cotan = cotan_ref[...].astype(f32)
    grad_norm = cotan * gate
    mean = jnp.mean(grad_norm * normed, axis=1, keepdims=True)
    grad_ref[...] = (row_scale * (grad_norm - normed * mean)).astype(bf16)
    out_ref[...] = (gate * normed).astype(bf16)
    gate_ref[...] = (cotan * normed).astype(bf16)


def slope_of(score):
    sig = sigmoid(score)
    return sig, sig * (1.0 + score * (1.0 - sig))


def wires_out(count, refs):
    return [refs[i : i + count] for i in range(0, len(refs), count)]


def query_kernel(count, blocks, see_ref, gq_ref, grad_ref, gate_ref, slots_ref, *refs):
    pairs, wires = refs[:blocks], wires_out(count, refs[blocks:])
    scale = HD ** (-0.5)
    see = see_ref[...]
    done = []
    for head in range(HEADS):
        keys = stack(pairs, head_cols(head, 1))
        _, slope = slope_of(dot_nt(gq_ref[:, head_cols(head, 1)], keys) * scale)
        att = dot_nt(grad_ref[:, head_cols(head)], stack(pairs, head_cols(head)))
        done.append((dot((att * slope * see).astype(bf16), keys) * scale).astype(bf16))
    parts_to_slots(slots_ref, [gate_ref[...], jnp.concatenate(done, axis=1)], wires)


def score_kernel(blocks, seen_ref, pair_ref, gq_ref, grad_ref, *refs):
    queries, (weight_ref, slope_ref, value_sum_ref, key_sum_ref) = refs[: blocks - 1], refs[blocks - 1 :]
    rows = pair_ref.shape[0]
    scale = HD ** (-0.5)
    seen = seen_ref[...]
    for head in range(HEADS):
        own = gq_ref[:, head_cols(head, 1)]
        query = jnp.concatenate([own, stack(queries, head_cols(head))], axis=0)
        score = dot_nt(pair_ref[:, head_cols(head, 1)], query) * scale
        sig, slope = slope_of(score)
        weight = (score * sig * seen).astype(bf16)
        slope = slope * seen
        grad = grad_ref[:, head_cols(head)]
        att = dot_nt(pair_ref[:, head_cols(head)], grad)
        value_sum_ref[:, head_cols(head)] = dot(weight[:, :rows], grad)
        key_sum_ref[:, head_cols(head)] = dot((att * slope[:, :rows]).astype(bf16), own)
        weight_ref[head] = weight[:, rows:]
        slope_ref[head] = slope[:, rows:]


def key_kernel(count, blocks, pair_ref, slots_ref, weight_ref, slope_ref, *refs):
    later = blocks - 1
    value_sum_ref, key_sum_ref = refs[:2]
    queries, grads = refs[2 : 2 + later], refs[2 + later : 2 + 2 * later]
    wires = wires_out(count, refs[2 + 2 * later :])
    scale = HD ** (-0.5)
    values, keys = [], []
    for head in range(HEADS):
        cols = head_cols(head)
        grad = stack(grads, cols)
        grad_score = (dot_nt(pair_ref[:, cols], grad) * slope_ref[head]).astype(bf16)
        value = dot(weight_ref[head], grad) + value_sum_ref[:, cols]
        key = dot(grad_score, stack(queries, cols)) + key_sum_ref[:, cols]
        values.append(value.astype(bf16))
        keys.append((key * scale).astype(bf16))
    parts = [jnp.concatenate(one, axis=1) for one in (values, keys)]
    parts_to_slots(slots_ref, parts, wires)


def owner_term(parts, refs, slope_ref, w_ref):
    width = HEADS * HD
    grad_pre = (unfold(refs).astype(f32) * slope_ref[...]).astype(bf16)
    term = None
    for i, part in enumerate(parts):
        one = dot_nt(
            grad_pre[:, i * width : (i + 1) * width], w_ref[:, part * width : (part + 1) * width]
        )
        term = one if term is None else term + one
    return term


def term_kernel(parts, slope_ref, w_ref, *refs):
    refs[-1][...] = owner_term(parts, refs[:-1], slope_ref, w_ref)


def last_term_kernel(count, parts, slope_ref, w_ref, *refs):
    ins, others, outs = refs[:count], refs[count:-count], refs[-count:]
    term = owner_term(parts, ins, slope_ref, w_ref)
    for other_ref in others:
        term = term + other_ref[...]
    fold(term.astype(bf16), outs)


def leave_kernel(count, rows_ref, events_ref, gain_ref, *refs):
    matrices = [rows_ref[i] for i in range(1 + FOLD)]
    wires = wires_out(count, refs[:-1])
    scaled = sum(from_slots(matrices, wire) for wire in wires) * gain_of(gain_ref)
    events = events_ref[...].astype(f32)
    row_inv = lax.rsqrt(jnp.mean(events * events, axis=1, keepdims=True) + eps)
    normed = events * row_inv
    mean = jnp.mean(scaled * normed, axis=1, keepdims=True)
    refs[-1][...] = (row_inv * (scaled - normed * mean)).astype(bf16)


def exchange(blocks):
    done = exchanged(blocks)
    if 1 < len(blocks) < lax.axis_size("user"):
        others = jnp.concatenate([block[MAIN:] for block in done], axis=0)
        done += [lax.ppermute(others, "user", [(i, i ^ 1) for i in range(lax.axis_size("user"))])]
    return done


def exchanged(blocks):
    count = lax.axis_size("user")
    if len(blocks) == 1:
        wire = blocks[0].reshape(-1, MAIN, blocks[0].shape[1])
        done = lax.all_to_all(wire, "user", split_axis=0, concat_axis=0, tiled=True)
        return [done.reshape(blocks[0].shape)]
    done = list(blocks)
    merged = count // len(blocks)
    for k in range(1, len(blocks)):
        done[k] = lax.ppermute(blocks[k], "user", [(i, i ^ (merged * k)) for i in range(count)])
    return done


def shifted(block, distance):
    count = lax.axis_size("seq")
    route = [((i - distance) % count, i) for i in range(count)]
    return lax.ppermute(block, "seq", route)


def wires_of(boxes):
    cols = boxes[0].shape[1]
    return [jnp.stack([box.reshape(SCEN, MAIN, cols) for box in boxes], axis=1).reshape(-1, cols)]


def slices_of(split, box):
    cols = box.shape[1]
    blocks = box.reshape(SCEN, split, MAIN, cols)
    return [blocks[:, i].reshape(-1, cols) for i in range(split)]


def shards(events, scenario, lengths, offsets, gain, w_proj, cotangent):
    n_seq = lax.axis_size("seq")
    n_user = lax.axis_size("user")
    split = n_user // SCEN
    rows, feats = events.shape[1:]
    width = HEADS * HD
    longest = n_seq * rows // 2
    reach = min(REACH, n_seq - 1, (longest - 2) // rows + 1)
    blocks = reach + 1
    direct = split == 1
    senders = SCEN if direct else 1

    def wire(rows, cols, merged=1):
        count = rows // (MAIN * merged) if direct else 1
        return [shape((rows // count, cols * (FOLD + 1) // FOLD), bf16)] * count

    slots = wire(SCEN * MAIN, feats)
    matrices = shape((1 + FOLD, rows, SCEN * MAIN), bf16)
    events, w_local, cotan = events[0], w_proj[0], cotangent[0]
    gain = gain.reshape(-1, LANES)

    to_slot, *outbox = call(
        functools.partial(enter_kernel, direct),
        [matrices] + slots,
        [events, gain, scenario],
        [pltpu.HBM] * 3,
        [
            pltpu.VMEM(events.shape, bf16),
            pltpu.VMEM(gain.shape, f32),
            pltpu.VMEM(scenario.shape, jnp.int32),
            pltpu.SemaphoreType.DMA((3,)),
        ],
    )
    inbound = exchange(outbox if direct else wires_of(outbox * split))
    small = jnp.concatenate([lengths, offsets, scenario], axis=1)
    w_local, to_row, see, seen = call(
        functools.partial(mask_kernel, direct, blocks, lengths.shape[1]),
        [shape(w_local.shape, bf16), matrices] + [shape((rows, blocks * rows), f32)] * 2,
        [w_local, small],
        [pltpu.HBM],
        [pltpu.SemaphoreType.DMA((4,))],
    )

    def project(parts, merged=1):
        cols = len(parts) * width
        *box, slope = call(
            functools.partial(project_kernel, senders, parts),
            wire(n_user * MAIN, cols, merged) + [shape((n_user * CAP, cols), f32)],
            [w_local] + inbound,
        )
        return exchange(box), slope

    def rows_of(box):
        cols = box[0].shape[1] * FOLD // (FOLD + 1)
        return call(rows_kernel, [shape((rows, cols), bf16)], [to_row] + box)[0]

    if direct:
        pair_parts, query_parts = (1, 3), (0, 2)
        pair_back, pair_slope = project(pair_parts)
        query_back, query_slope = project(query_parts)
        pair_own = rows_of(pair_back)
        gq = rows_of(query_back)
    else:
        (box,), slope = project((0,))
        gate, value, query, key = [rows_of([part]) for part in slices_of(split, box)]
        pair_own = jnp.concatenate([value, key], axis=1)
        gq = jnp.concatenate([gate, query], axis=1)
    pairs = [pair_own] + [shifted(pair_own, d) for d in range(1, blocks)]
    query_own = gq[:, width:]
    queries = [shifted(query_own, -d) for d in range(1, blocks)]
    half = shape((rows, width), bf16)
    output, grad_own, grad_gate = call(
        functools.partial(forward_kernel, blocks), [half] * 3, [see, gq, cotan] + pairs
    )
    grads = [shifted(grad_own, -d) for d in range(1, blocks)]

    def boxes(merged=1):
        cols = 2 * width if direct else width
        return wire(SCEN * MAIN, cols, merged) * (1 if direct else 2)

    query_grad = call(
        functools.partial(query_kernel, len(boxes(2)) if direct else 1, blocks),
        boxes(2),
        [see, gq, grad_own, grad_gate, to_slot] + pairs,
    )
    each = (HEADS, rows, reach * rows)
    scores = call(
        functools.partial(score_kernel, blocks),
        [shape(each, bf16), shape(each, f32)] + [shape((rows, width), f32)] * 2,
        [seen, pair_own, gq, grad_own] + queries,
    )
    pair_grad = call(
        functools.partial(key_kernel, senders, blocks),
        boxes(),
        [pair_own, to_slot, *scores] + queries + grads,
    )
    term = shape((n_user * CAP, feats), f32)
    if direct:
        (query_term,) = call(
            functools.partial(term_kernel, query_parts),
            [term],
            [query_slope, w_local] + exchange(query_grad),
        )
        last_parts, last = pair_parts, [pair_slope, w_local] + exchange(pair_grad) + [query_term]
    else:
        order = [query_grad[0], pair_grad[0], query_grad[1], pair_grad[1]]
        last_parts, last = (0,), [slope, w_local] + exchange(wires_of(order))
    term_box = call(
        functools.partial(last_term_kernel, senders, last_parts), wire(n_user * MAIN, feats), last
    )
    term_back = exchange(term_box)
    (grad_events,) = call(
        functools.partial(leave_kernel, senders),
        [shape((rows, feats), bf16)],
        [to_row, events, gain] + (term_back if direct else slices_of(split, term_back[0])),
    )
    return output[None], grad_events[None]


def solution(mesh):
    placed = (
        P("user", "seq", None),
        P("user", "seq"),
        P("user", None),
        P("user", None),
        P(),
        P("user", None, None),
        P("user", "seq", None),
    )
    return jax.shard_map(
        shards,
        mesh=mesh,
        in_specs=placed,
        out_specs=(P("user", "seq", None), P("user", "seq", None)),
        check_vma=False,
    )
```

```python
import functools

import jax
import jax.numpy as jnp
from jax import lax
from jax.experimental import pallas as pl
from jax.experimental.pallas import tpu as pltpu
from jax.sharding import PartitionSpec as P


HEADS = 6
HD = 128
SCEN = 8
MB = 128
CAP = 20
REACH = 4

MAIN = 16
EXTRA = CAP - MAIN
FOLD = MAIN // EXTRA

VMEM_LIMIT = 24 << 20
LANES = 128

eps = 1e-05
f32 = jnp.float32
bf16 = jnp.bfloat16
NT = (((1,), (1,)), ((), ()))


def call(kernel, outs, operands, spaces=(), scratch=(), flops=1 << 24, limit=VMEM_LIMIT):
    spaces = list(spaces) + [pltpu.VMEM] * (len(operands) - len(spaces))
    moved = sum(o.size * o.dtype.itemsize for o in list(outs) + list(operands))
    operands = [
        pltpu.with_memory_space_constraint(operand, space) if space == pltpu.HBM else operand
        for operand, space in zip(operands, spaces)
    ]
    return pl.pallas_call(
        kernel,
        out_shape=tuple(outs),
        in_specs=[pl.BlockSpec(memory_space=space) for space in spaces],
        out_specs=tuple(pl.BlockSpec(memory_space=pltpu.VMEM) for _ in outs),
        scratch_shapes=list(scratch),
        cost_estimate=pl.CostEstimate(flops=flops, bytes_accessed=moved, transcendentals=0),
        compiler_params=pltpu.CompilerParams(vmem_limit_bytes=limit),
    )(*operands)


def shape(dims, dtype):
    return jax.ShapeDtypeStruct(dims, dtype)


def dot(a, b):
    return jnp.dot(a, b, preferred_element_type=f32)


def dot_nt(a, b):
    return lax.dot_general(a, b, NT, preferred_element_type=f32)


def sigmoid(v):
    return 0.5 * jnp.tanh(0.5 * v) + 0.5


def iotas(rows, cols):
    return (
        lax.broadcasted_iota(jnp.int32, (rows, cols), 0),
        lax.broadcasted_iota(jnp.int32, (rows, cols), 1),
    )


def hot(condition):
    return jnp.where(condition, 1.0, 0.0).astype(bf16)


def load(refs, cols):
    if swapped(refs):
        parts = []
        for i, ref in enumerate(refs[:-1]):
            parts += [ref[:MAIN, cols], refs[-1][i * MAIN : (i + 1) * MAIN, cols]]
    else:
        parts = [ref[:, cols] for ref in refs]
    return parts[0] if len(parts) == 1 else jnp.concatenate(parts, axis=0)


def swapped(refs):
    return len(refs) > 1 and refs[0].shape[0] == 2 * MAIN


def rows_in(refs):
    return 2 * refs[-1].shape[0] if swapped(refs) else sum(ref.shape[0] for ref in refs)


def store(refs, cols, value):
    rows = refs[0].shape[0]
    for i, ref in enumerate(refs):
        ref[:, cols] = value[i * rows : (i + 1) * rows]


def main_cols(refs):
    return refs[0].shape[1] * FOLD // (FOLD + 1)


def slot_matrices(scen_row, by_slot):
    rows = scen_row.shape[1]
    down, along = iotas(rows, rows)
    scen_b = jnp.broadcast_to(scen_row.astype(f32), (rows, rows))
    scen_col = jnp.sum(jnp.where(down == along, scen_b, 0.0), axis=1, keepdims=True)
    same = scen_b == scen_col
    if by_slot:
        scen = scen_row.astype(f32)
        rank = jnp.sum(jnp.where(same & (down < along), 1.0, 0.0), axis=0, keepdims=True)
        down, along = iotas(SCEN * MAIN, rows)
        slot = down.astype(f32)
    else:
        scen = scen_col
        rank = jnp.sum(jnp.where(same & (along < down), 1.0, 0.0), axis=1, keepdims=True)
        down, along = iotas(rows, SCEN * MAIN)
        slot = along.astype(f32)
    main = jnp.where(rank < MAIN, scen * MAIN + rank, -1.0)
    out = [hot(slot == main)]
    for piece in range(FOLD):
        extra = jnp.where(rank >= MAIN, scen * MAIN + EXTRA * piece + (rank - MAIN), -1.0)
        out.append(hot(slot == extra))
    return out


def to_slots(matrices, value, refs):
    cols = value.shape[1]
    piece = cols // FOLD
    store(refs, slice(0, cols), dot(matrices[0], value).astype(bf16))
    extra = dot(matrices[1], value[:, :piece])
    for part in range(1, FOLD):
        extra = extra + dot(matrices[1 + part], value[:, part * piece : (part + 1) * piece])
    store(refs, slice(cols, cols + piece), extra.astype(bf16))


def from_slots(matrices, refs):
    cols = main_cols(refs)
    piece = cols // FOLD
    extra = load(refs, slice(cols, cols + piece))
    out = []
    for part in range(FOLD):
        left = jnp.concatenate([matrices[0], matrices[1 + part]], axis=1)
        right = jnp.concatenate([load(refs, slice(part * piece, (part + 1) * piece)), extra], axis=0)
        out.append(dot(left, right))
    return jnp.concatenate(out, axis=1)


def parts_to_slots(slots_ref, parts, wires):
    matrices = [slots_ref[i] for i in range(1 + FOLD)]
    if len(wires) == 1:
        parts = [jnp.concatenate(parts, axis=1)]
    for part, refs in zip(parts, wires):
        to_slots(matrices, part, refs)


def extra_matrix(count, part, by_row):
    if by_row:
        down, along = iotas(count * EXTRA, count * MAIN)
    else:
        along, down = iotas(count * MAIN, count * EXTRA)
    group = sum((down >= EXTRA * i).astype(jnp.int32) for i in range(1, count))
    return hot(along == down + group * (MAIN - EXTRA) + EXTRA * part)


def unfold(refs):
    count = rows_in(refs) // MAIN
    cols = main_cols(refs)
    extra = load(refs, slice(cols, cols + cols // FOLD))
    pieces = [dot(extra_matrix(count, part, True), extra) for part in range(FOLD)]
    extra = jnp.concatenate(pieces, axis=1).astype(bf16)
    return jnp.concatenate([load(refs, slice(0, cols)), extra], axis=0)


def fold(value, refs):
    rows, cols = sum(ref.shape[0] for ref in refs), value.shape[1]
    count = rows // MAIN
    piece = cols // FOLD
    store(refs, slice(0, cols), value[:rows])
    extra = sum(
        dot(extra_matrix(count, part, False), value[rows:, part * piece : (part + 1) * piece])
        for part in range(FOLD)
    )
    store(refs, slice(cols, cols + piece), extra.astype(bf16))


def own_scenarios(scen_ref, direct):
    return scen_ref[...] ^ lax.axis_index("user") if direct else scen_ref[...]


def gain_of(gain_ref):
    return jnp.concatenate([gain_ref[i : i + 1] for i in range(gain_ref.shape[0])], axis=1)


def enter_kernel(direct, events_hbm, gain_hbm, scen_hbm, slots_ref, *refs):
    events_ref, gain_ref, scen_ref, sems = refs[-4:]
    refs = refs[:-4]
    loads = [
        pltpu.make_async_copy(source, target, sems.at[i])
        for i, (source, target) in enumerate(
            [(events_hbm, events_ref), (gain_hbm, gain_ref), (scen_hbm, scen_ref)]
        )
    ]
    for load_ in reversed(loads):
        load_.start()
    loads[2].wait()
    matrices = slot_matrices(own_scenarios(scen_ref, direct), True)
    for i, matrix in enumerate(matrices):
        slots_ref[i] = matrix
    loads[1].wait()
    loads[0].wait()
    events = events_ref[...].astype(f32)
    row_inv = lax.rsqrt(jnp.mean(events * events, axis=1, keepdims=True) + eps)
    normed = (events * row_inv * gain_of(gain_ref)).astype(bf16)
    to_slots(matrices, normed, refs)


def history_of(pos, ends):
    return sum((pos >= end).astype(jnp.int32) for end in ends)


def limit_of(history, limits):
    return sum(jnp.where(history == i, limit, 0) for i, limit in enumerate(limits))


def mask_kernel(
    direct, blocks, histories, w_hbm, small_ref, w_ref, rows_ref, see_ref, seen_ref, sems
):
    count = sems.shape[0]
    depth = w_ref.shape[0] // count
    loads = [
        pltpu.make_async_copy(
            w_hbm.at[pl.ds(i * depth, depth)], w_ref.at[pl.ds(i * depth, depth)], sems.at[i]
        )
        for i in range(count)
    ]
    for load_ in loads:
        load_.start()
    for i, matrix in enumerate(
        slot_matrices(own_scenarios(small_ref.at[:, 2 * histories :], direct), False)
    ):
        rows_ref[i] = matrix
    rows = see_ref.shape[0]
    ends, total = [], 0
    for i in range(histories):
        total = total + small_ref[:, i : i + 1]
        ends.append(total)
    limits = [small_ref[:, i : i + 1] for i in range(histories, 2 * histories)]
    first = lax.axis_index("seq") * rows
    shift = MB.bit_length() - 1

    def visible(query, key):
        query_hist, key_hist = history_of(query, ends), history_of(key, ends)
        near = (query >> shift) - (key >> shift) <= limit_of(query_hist, limits)
        return jnp.where((query_hist == key_hist) & (key <= query) & (key >= 0) & near, 1.0, 0.0)

    down = lax.broadcasted_iota(jnp.int32, (rows, rows), 0)
    along = lax.broadcasted_iota(jnp.int32, (rows, rows), 1)
    for block in range(blocks):
        span = slice(block * rows, (block + 1) * rows)
        see_ref[:, span] = visible(first + down, first - block * rows + along)
        seen_ref[:, span] = visible(first + block * rows + along, first + down)
    for load_ in loads:
        load_.wait()


def project_kernel(count, parts, w_ref, *refs):
    ins, outs, slope_ref = refs[:count], refs[count:-1], refs[-1]
    rows = unfold(ins)
    width = HEADS * HD
    done = []
    for i, part in enumerate(parts):
        pre = dot(rows, w_ref[:, part * width : (part + 1) * width])
        sig = sigmoid(pre)
        slope_ref[:, i * width : (i + 1) * width] = sig * (1.0 + pre * (1.0 - sig))
        done.append((pre * sig).astype(bf16))
    fold(jnp.concatenate(done, axis=1), outs)


def rows_kernel(outs, rows_ref, *refs):
    matrices = [rows_ref[i] for i in range(1 + FOLD)]
    rows = from_slots(matrices, refs[:-outs]).astype(bf16)
    width = rows.shape[1] // outs
    for i, ref in enumerate(refs[-outs:]):
        ref[...] = rows[:, i * width : (i + 1) * width]


def head_cols(head):
    return slice(head * HD, (head + 1) * HD)


ACROSS = [(0, 1), (1, 0), (2, 3), (3, 2)]


def by_corner(blocks):
    return lax.axis_size("seq") == 4 and blocks == 3


def shifted_pairs(value, key, blocks):
    if not by_corner(blocks):
        return [[one] + [shifted(one, d) for d in range(1, blocks)] for one in (value, key)]
    key_far = shifted(key, 2)
    value_near = shifted(value, 1)
    value_far = shifted(value, 2)
    key_near = lax.ppermute(key, "seq", ACROSS)
    handed = lax.ppermute(key_far, "seq", ACROSS)
    return [value, value_near, value_far], [key, key_near, key_far, handed]


def shifted_queries(query, blocks):
    if not by_corner(blocks):
        return [shifted(query, -d) for d in range(1, blocks)]
    far = shifted(query, -2)
    near = lax.ppermute(query, "seq", ACROSS)
    return [near, far, lax.ppermute(far, "seq", ACROSS)]


def stack(refs, cols, blocks, corner=0):
    parts = [ref[:, cols] for ref in refs[:blocks]]
    if len(refs) > blocks:
        at = 0 if corner == 1 else 1
        parts[at] = jnp.where(lax.axis_index("seq") == corner, refs[blocks][:, cols], parts[at])
    return jnp.concatenate(parts, axis=0)


def forward_kernel(blocks, see_ref, gate_in_ref, query_ref, cotan_ref, *refs):
    out_ref, grad_ref, gate_ref = refs[-3:]
    values, keys = refs[:blocks], refs[blocks:-3]
    scale = HD ** (-0.5)
    see = see_ref[...]
    done = []
    for head in range(HEADS):
        cols = head_cols(head)
        score = dot_nt(query_ref[:, cols], stack(keys, cols, blocks, 2)) * scale
        weight = (score * sigmoid(score) * see).astype(bf16)
        done.append(dot(weight, stack(values, cols, blocks)))
    mixed = jnp.concatenate(done, axis=1)
    row_scale = lax.rsqrt(jnp.mean(mixed * mixed, axis=1, keepdims=True) + eps)
    normed = mixed * row_scale
    gate = gate_in_ref[...].astype(f32)
    cotan = cotan_ref[...].astype(f32)
    grad_norm = cotan * gate
    mean = jnp.mean(grad_norm * normed, axis=1, keepdims=True)
    grad_ref[...] = (row_scale * (grad_norm - normed * mean)).astype(bf16)
    out_ref[...] = (gate * normed).astype(bf16)
    gate_ref[...] = (cotan * normed).astype(bf16)


def slope_of(score):
    sig = sigmoid(score)
    return sig, sig * (1.0 + score * (1.0 - sig))


def wires_out(count, refs):
    return [refs[i : i + count] for i in range(0, len(refs), count)]


def query_kernel(count, total, blocks, see_ref, query_ref, grad_ref, gate_ref, slots_ref, *refs):
    wires = wires_out(count, refs[-total:])
    values, keys = refs[:blocks], refs[blocks:-total]
    scale = HD ** (-0.5)
    see = see_ref[...]
    done = []
    for head in range(HEADS):
        cols = head_cols(head)
        key = stack(keys, cols, blocks, 2)
        _, slope = slope_of(dot_nt(query_ref[:, cols], key) * scale)
        att = dot_nt(grad_ref[:, cols], stack(values, cols, blocks))
        done.append((dot((att * slope * see).astype(bf16), key) * scale).astype(bf16))
    parts_to_slots(slots_ref, [gate_ref[...], jnp.concatenate(done, axis=1)], wires)


def score_kernel(blocks, seen_ref, value_ref, key_ref, query_ref, grad_ref, *refs):
    queries, (weight_ref, slope_ref, value_sum_ref, key_sum_ref) = refs[:-4], refs[-4:]
    rows = key_ref.shape[0]
    scale = HD ** (-0.5)
    seen = seen_ref[...]
    for head in range(HEADS):
        own = query_ref[:, head_cols(head)]
        query = jnp.concatenate([own, stack(queries, head_cols(head), blocks - 1, 1)], axis=0)
        score = dot_nt(key_ref[:, head_cols(head)], query) * scale
        sig, slope = slope_of(score)
        weight = (score * sig * seen).astype(bf16)
        slope = slope * seen
        grad = grad_ref[:, head_cols(head)]
        att = dot_nt(value_ref[:, head_cols(head)], grad)
        value_sum_ref[:, head_cols(head)] = dot(weight[:, :rows], grad)
        key_sum_ref[:, head_cols(head)] = dot((att * slope[:, :rows]).astype(bf16), own)
        weight_ref[head] = weight[:, rows:]
        slope_ref[head] = slope[:, rows:]


def key_kernel(count, total, blocks, value_ref, slots_ref, weight_ref, slope_ref, *refs):
    later = blocks - 1
    value_sum_ref, key_sum_ref = refs[:2]
    grads, queries = refs[2 : 2 + later], refs[2 + later : -total]
    wires = wires_out(count, refs[-total:])
    scale = HD ** (-0.5)
    values, keys = [], []
    for head in range(HEADS):
        cols = head_cols(head)
        grad = stack(grads, cols, later)
        grad_score = (dot_nt(value_ref[:, cols], grad) * slope_ref[head]).astype(bf16)
        value = dot(weight_ref[head], grad) + value_sum_ref[:, cols]
        key = dot(grad_score, stack(queries, cols, later, 1)) + key_sum_ref[:, cols]
        values.append(value.astype(bf16))
        keys.append((key * scale).astype(bf16))
    parts = [jnp.concatenate(one, axis=1) for one in (values, keys)]
    parts_to_slots(slots_ref, parts, wires)


def owner_term(parts, refs, slope_ref, w_ref):
    width = HEADS * HD
    grad_pre = (unfold(refs).astype(f32) * slope_ref[...]).astype(bf16)
    term = None
    for i, part in enumerate(parts):
        one = dot_nt(
            grad_pre[:, i * width : (i + 1) * width], w_ref[:, part * width : (part + 1) * width]
        )
        term = one if term is None else term + one
    return term


def term_kernel(parts, slope_ref, w_ref, *refs):
    refs[-1][...] = owner_term(parts, refs[:-1], slope_ref, w_ref)


def last_term_kernel(count, parts, slope_ref, w_ref, *refs):
    ins, others, outs = refs[:count], refs[count:-count], refs[-count:]
    term = owner_term(parts, ins, slope_ref, w_ref)
    for other_ref in others:
        term = term + other_ref[...]
    fold(term.astype(bf16), outs)


def leave_kernel(count, rows_ref, events_ref, gain_ref, *refs):
    matrices = [rows_ref[i] for i in range(1 + FOLD)]
    wires = wires_out(count, refs[:-1])
    scaled = sum(from_slots(matrices, wire) for wire in wires) * gain_of(gain_ref)
    events = events_ref[...].astype(f32)
    row_inv = lax.rsqrt(jnp.mean(events * events, axis=1, keepdims=True) + eps)
    normed = events * row_inv
    mean = jnp.mean(scaled * normed, axis=1, keepdims=True)
    refs[-1][...] = (row_inv * (scaled - normed * mean)).astype(bf16)


def exchange(blocks):
    done = exchanged(blocks)
    if 1 < len(blocks) < lax.axis_size("user"):
        others = jnp.concatenate([block[MAIN:] for block in done], axis=0)
        done += [lax.ppermute(others, "user", [(i, i ^ 1) for i in range(lax.axis_size("user"))])]
    return done


def exchanged(blocks):
    count = lax.axis_size("user")
    if len(blocks) == 1:
        wire = blocks[0].reshape(-1, MAIN, blocks[0].shape[1])
        done = lax.all_to_all(wire, "user", split_axis=0, concat_axis=0, tiled=True)
        return [done.reshape(blocks[0].shape)]
    done = list(blocks)
    merged = count // len(blocks)
    for k in range(1, len(blocks)):
        done[k] = lax.ppermute(blocks[k], "user", [(i, i ^ (merged * k)) for i in range(count)])
    return done


def shifted(block, distance):
    count = lax.axis_size("seq")
    route = [((i - distance) % count, i) for i in range(count)]
    return lax.ppermute(block, "seq", route)


def wires_of(boxes):
    cols = boxes[0].shape[1]
    return [jnp.stack([box.reshape(SCEN, MAIN, cols) for box in boxes], axis=1).reshape(-1, cols)]


def slices_of(split, box):
    cols = box.shape[1]
    blocks = box.reshape(SCEN, split, MAIN, cols)
    return [blocks[:, i].reshape(-1, cols) for i in range(split)]


def shards(events, scenario, lengths, offsets, gain, w_proj, cotangent):
    n_seq = lax.axis_size("seq")
    n_user = lax.axis_size("user")
    split = n_user // SCEN
    rows, feats = events.shape[1:]
    width = HEADS * HD
    longest = n_seq * rows // 2
    reach = min(REACH, n_seq - 1, (longest - 2) // rows + 1)
    blocks = reach + 1
    direct = split == 1
    senders = SCEN if direct else 1

    def wire(rows, cols, merged=1):
        count = rows // (MAIN * merged) if direct else 1
        return [shape((rows // count, cols * (FOLD + 1) // FOLD), bf16)] * count

    slots = wire(SCEN * MAIN, feats)
    matrices = shape((1 + FOLD, rows, SCEN * MAIN), bf16)
    events, w_local, cotan = events[0], w_proj[0], cotangent[0]
    gain = gain.reshape(-1, LANES)

    to_slot, *outbox = call(
        functools.partial(enter_kernel, direct),
        [matrices] + slots,
        [events, gain, scenario],
        [pltpu.HBM] * 3,
        [
            pltpu.VMEM(events.shape, bf16),
            pltpu.VMEM(gain.shape, f32),
            pltpu.VMEM(scenario.shape, jnp.int32),
            pltpu.SemaphoreType.DMA((3,)),
        ],
    )
    inbound = exchange(outbox if direct else wires_of(outbox * split))
    small = jnp.concatenate([lengths, offsets, scenario], axis=1)
    w_local, to_row, see, seen = call(
        functools.partial(mask_kernel, direct, blocks, lengths.shape[1]),
        [shape(w_local.shape, bf16), matrices] + [shape((rows, blocks * rows), f32)] * 2,
        [w_local, small],
        [pltpu.HBM],
        [pltpu.SemaphoreType.DMA((4,))],
    )

    def project(parts, merged=1):
        cols = len(parts) * width
        *box, slope = call(
            functools.partial(project_kernel, senders, parts),
            wire(n_user * MAIN, cols, merged) + [shape((n_user * CAP, cols), f32)],
            [w_local] + inbound,
        )
        return exchange(box), slope

    def rows_of(box, parts=2):
        outs = [shape((rows, width), bf16)] * parts
        return call(functools.partial(rows_kernel, parts), outs, [to_row] + box)

    if direct:
        pair_parts, query_parts = (1, 3), (0, 2)
        pair_back, pair_slope = project(pair_parts)
        query_back, query_slope = project(query_parts)
        value, key = rows_of(pair_back)
        gate, query = rows_of(query_back)
    else:
        (box,), slope = project((0,))
        gate, value, query, key = [rows_of([part], 1)[0] for part in slices_of(split, box)]
    values, keys = shifted_pairs(value, key, blocks)
    queries = shifted_queries(query, blocks)
    half = shape((rows, width), bf16)
    output, grad_own, grad_gate = call(
        functools.partial(forward_kernel, blocks),
        [half] * 3,
        [see, gate, query, cotan] + values + keys,
    )
    grads = [shifted(grad_own, -d) for d in range(1, blocks)]

    def boxes(merged=1):
        cols = 2 * width if direct else width
        return wire(SCEN * MAIN, cols, merged) * (1 if direct else 2)

    query_grad = call(
        functools.partial(query_kernel, len(boxes(2)) if direct else 1, len(boxes(2)), blocks),
        boxes(2),
        [see, query, grad_own, grad_gate, to_slot] + values + keys,
    )
    each = (HEADS, rows, reach * rows)
    scores = call(
        functools.partial(score_kernel, blocks),
        [shape(each, bf16), shape(each, f32)] + [shape((rows, width), f32)] * 2,
        [seen, value, key, query, grad_own] + queries,
    )
    pair_grad = call(
        functools.partial(key_kernel, senders, len(boxes()), blocks),
        boxes(),
        [value, to_slot, *scores] + grads + queries,
    )
    term = shape((n_user * CAP, feats), f32)
    if direct:
        (query_term,) = call(
            functools.partial(term_kernel, query_parts),
            [term],
            [query_slope, w_local] + exchange(query_grad),
        )
        last_parts, last = pair_parts, [pair_slope, w_local] + exchange(pair_grad) + [query_term]
    else:
        order = [query_grad[0], pair_grad[0], query_grad[1], pair_grad[1]]
        last_parts, last = (0,), [slope, w_local] + exchange(wires_of(order))
    term_box = call(
        functools.partial(last_term_kernel, senders, last_parts), wire(n_user * MAIN, feats), last
    )
    term_back = exchange(term_box)
    (grad_events,) = call(
        functools.partial(leave_kernel, senders),
        [shape((rows, feats), bf16)],
        [to_row, events, gain] + (term_back if direct else slices_of(split, term_back[0])),
    )
    return output[None], grad_events[None]


def solution(mesh):
    placed = (
        P("user", "seq", None),
        P("user", "seq"),
        P("user", None),
        P("user", None),
        P(),
        P("user", None, None),
        P("user", "seq", None),
    )
    return jax.shard_map(
        shards,
        mesh=mesh,
        in_specs=placed,
        out_specs=(P("user", "seq", None), P("user", "seq", None)),
        check_vma=False,
    )
```

```python
import functools

import jax
import jax.numpy as jnp
from jax import lax
from jax.experimental import pallas as pl
from jax.experimental.pallas import tpu as pltpu
from jax.sharding import PartitionSpec as P


HEADS = 6
HD = 128
SCEN = 8
MB = 128
CAP = 20
REACH = 4

MAIN = 16
EXTRA = CAP - MAIN
FOLD = MAIN // EXTRA

VMEM_LIMIT = 24 << 20
LANES = 128

eps = 1e-05
f32 = jnp.float32
bf16 = jnp.bfloat16
NT = (((1,), (1,)), ((), ()))


def call(kernel, outs, operands, spaces=(), scratch=(), flops=1 << 24, limit=VMEM_LIMIT):
    spaces = list(spaces) + [pltpu.VMEM] * (len(operands) - len(spaces))
    moved = sum(o.size * o.dtype.itemsize for o in list(outs) + list(operands))
    operands = [
        pltpu.with_memory_space_constraint(operand, space) if space == pltpu.HBM else operand
        for operand, space in zip(operands, spaces)
    ]
    return pl.pallas_call(
        kernel,
        out_shape=tuple(outs),
        in_specs=[pl.BlockSpec(memory_space=space) for space in spaces],
        out_specs=tuple(pl.BlockSpec(memory_space=pltpu.VMEM) for _ in outs),
        scratch_shapes=list(scratch),
        cost_estimate=pl.CostEstimate(flops=flops, bytes_accessed=moved, transcendentals=0),
        compiler_params=pltpu.CompilerParams(vmem_limit_bytes=limit),
    )(*operands)


def shape(dims, dtype):
    return jax.ShapeDtypeStruct(dims, dtype)


def dot(a, b):
    return jnp.dot(a, b, preferred_element_type=f32)


def dot_nt(a, b):
    return lax.dot_general(a, b, NT, preferred_element_type=f32)


def sigmoid(v):
    return 0.5 * jnp.tanh(0.5 * v) + 0.5


def iotas(rows, cols):
    return (
        lax.broadcasted_iota(jnp.int32, (rows, cols), 0),
        lax.broadcasted_iota(jnp.int32, (rows, cols), 1),
    )


def hot(condition):
    return jnp.where(condition, 1.0, 0.0).astype(bf16)


def load(refs, cols):
    if swapped(refs):
        parts = []
        for i, ref in enumerate(refs[:-1]):
            parts += [ref[:MAIN, cols], refs[-1][i * MAIN : (i + 1) * MAIN, cols]]
    else:
        parts = [ref[:, cols] for ref in refs]
    return parts[0] if len(parts) == 1 else jnp.concatenate(parts, axis=0)


def swapped(refs):
    return len(refs) > 1 and refs[0].shape[0] == 2 * MAIN


def rows_in(refs):
    return 2 * refs[-1].shape[0] if swapped(refs) else sum(ref.shape[0] for ref in refs)


def store(refs, cols, value):
    rows = refs[0].shape[0]
    for i, ref in enumerate(refs):
        ref[:, cols] = value[i * rows : (i + 1) * rows]


def main_cols(refs):
    return refs[0].shape[1] * FOLD // (FOLD + 1)


def slot_matrices(scen_row, by_slot):
    rows = scen_row.shape[1]
    down, along = iotas(rows, rows)
    scen_b = jnp.broadcast_to(scen_row.astype(f32), (rows, rows))
    scen_col = jnp.sum(jnp.where(down == along, scen_b, 0.0), axis=1, keepdims=True)
    same = scen_b == scen_col
    if by_slot:
        scen = scen_row.astype(f32)
        rank = jnp.sum(jnp.where(same & (down < along), 1.0, 0.0), axis=0, keepdims=True)
        down, along = iotas(SCEN * MAIN, rows)
        slot = down.astype(f32)
    else:
        scen = scen_col
        rank = jnp.sum(jnp.where(same & (along < down), 1.0, 0.0), axis=1, keepdims=True)
        down, along = iotas(rows, SCEN * MAIN)
        slot = along.astype(f32)
    main = jnp.where(rank < MAIN, scen * MAIN + rank, -1.0)
    out = [hot(slot == main)]
    for piece in range(FOLD):
        extra = jnp.where(rank >= MAIN, scen * MAIN + EXTRA * piece + (rank - MAIN), -1.0)
        out.append(hot(slot == extra))
    return out


def to_slots(matrices, value, refs):
    cols = value.shape[1]
    piece = cols // FOLD
    store(refs, slice(0, cols), dot(matrices[0], value).astype(bf16))
    extra = dot(matrices[1], value[:, :piece])
    for part in range(1, FOLD):
        extra = extra + dot(matrices[1 + part], value[:, part * piece : (part + 1) * piece])
    store(refs, slice(cols, cols + piece), extra.astype(bf16))


def from_slots(matrices, refs):
    cols = main_cols(refs)
    piece = cols // FOLD
    extra = load(refs, slice(cols, cols + piece))
    out = []
    for part in range(FOLD):
        left = jnp.concatenate([matrices[0], matrices[1 + part]], axis=1)
        right = jnp.concatenate([load(refs, slice(part * piece, (part + 1) * piece)), extra], axis=0)
        out.append(dot(left, right))
    return jnp.concatenate(out, axis=1)


def parts_to_slots(slots_ref, parts, wires):
    matrices = [slots_ref[i] for i in range(1 + FOLD)]
    if len(wires) == 1:
        parts = [jnp.concatenate(parts, axis=1)]
    for part, refs in zip(parts, wires):
        to_slots(matrices, part, refs)


def extra_matrix(count, part, by_row):
    if by_row:
        down, along = iotas(count * EXTRA, count * MAIN)
    else:
        along, down = iotas(count * MAIN, count * EXTRA)
    group = sum((down >= EXTRA * i).astype(jnp.int32) for i in range(1, count))
    return hot(along == down + group * (MAIN - EXTRA) + EXTRA * part)


def unfold(refs):
    count = rows_in(refs) // MAIN
    cols = main_cols(refs)
    extra = load(refs, slice(cols, cols + cols // FOLD))
    pieces = [dot(extra_matrix(count, part, True), extra) for part in range(FOLD)]
    extra = jnp.concatenate(pieces, axis=1).astype(bf16)
    return jnp.concatenate([load(refs, slice(0, cols)), extra], axis=0)


def fold(value, refs):
    rows, cols = sum(ref.shape[0] for ref in refs), value.shape[1]
    count = rows // MAIN
    piece = cols // FOLD
    store(refs, slice(0, cols), value[:rows])
    extra = sum(
        dot(extra_matrix(count, part, False), value[rows:, part * piece : (part + 1) * piece])
        for part in range(FOLD)
    )
    store(refs, slice(cols, cols + piece), extra.astype(bf16))


def own_scenarios(scen_ref, direct):
    return scen_ref[...] ^ lax.axis_index("user") if direct else scen_ref[...]


def gain_of(gain_ref):
    return jnp.concatenate([gain_ref[i : i + 1] for i in range(gain_ref.shape[0])], axis=1)


def enter_kernel(direct, events_hbm, gain_hbm, scen_hbm, slots_ref, *refs):
    events_ref, gain_ref, scen_ref, sems = refs[-4:]
    refs = refs[:-4]
    loads = [
        pltpu.make_async_copy(source, target, sems.at[i])
        for i, (source, target) in enumerate(
            [(events_hbm, events_ref), (gain_hbm, gain_ref), (scen_hbm, scen_ref)]
        )
    ]
    for load_ in reversed(loads):
        load_.start()
    loads[2].wait()
    matrices = slot_matrices(own_scenarios(scen_ref, direct), True)
    for i, matrix in enumerate(matrices):
        slots_ref[i] = matrix
    loads[1].wait()
    loads[0].wait()
    events = events_ref[...].astype(f32)
    row_inv = lax.rsqrt(jnp.mean(events * events, axis=1, keepdims=True) + eps)
    normed = (events * row_inv * gain_of(gain_ref)).astype(bf16)
    to_slots(matrices, normed, refs)


def history_of(pos, ends):
    return sum((pos >= end).astype(jnp.int32) for end in ends)


def limit_of(history, limits):
    return sum(jnp.where(history == i, limit, 0) for i, limit in enumerate(limits))


def mask_kernel(
    direct, blocks, histories, w_hbm, small_ref, w_ref, rows_ref, see_ref, seen_ref, sems
):
    count = sems.shape[0]
    depth = w_ref.shape[0] // count
    loads = [
        pltpu.make_async_copy(
            w_hbm.at[pl.ds(i * depth, depth)], w_ref.at[pl.ds(i * depth, depth)], sems.at[i]
        )
        for i in range(count)
    ]
    for load_ in loads:
        load_.start()
    for i, matrix in enumerate(
        slot_matrices(own_scenarios(small_ref.at[:, 2 * histories :], direct), False)
    ):
        rows_ref[i] = matrix
    rows = see_ref.shape[0]
    ends, total = [], 0
    for i in range(histories):
        total = total + small_ref[:, i : i + 1]
        ends.append(total)
    limits = [small_ref[:, i : i + 1] for i in range(histories, 2 * histories)]
    first = lax.axis_index("seq") * rows
    shift = MB.bit_length() - 1

    def visible(query, key):
        query_hist, key_hist = history_of(query, ends), history_of(key, ends)
        near = (query >> shift) - (key >> shift) <= limit_of(query_hist, limits)
        return jnp.where((query_hist == key_hist) & (key <= query) & (key >= 0) & near, 1.0, 0.0)

    down = lax.broadcasted_iota(jnp.int32, (rows, rows), 0)
    along = lax.broadcasted_iota(jnp.int32, (rows, rows), 1)
    for block in range(blocks):
        span = slice(block * rows, (block + 1) * rows)
        see_ref[:, span] = visible(first + down, first - block * rows + along)
        seen_ref[:, span] = visible(first + block * rows + along, first + down)
    for load_ in loads:
        load_.wait()


def project_kernel(count, parts, early, late, w_ref, *refs):
    ins, rest, kept_ref = refs[:count], refs[count:-1], refs[-1]
    if late:
        _, rest[-1][...] = slope_of(rest[0][...])
        rest = rest[1:-1]
    outs = rest
    rows = unfold(ins)
    width = HEADS * HD
    done = []
    for i, part in enumerate(parts):
        pre = dot(rows, w_ref[:, part * width : (part + 1) * width])
        sig = sigmoid(pre)
        cols = slice(i * width, (i + 1) * width)
        kept_ref[:, cols] = pre if early else sig * (1.0 + pre * (1.0 - sig))
        done.append((pre * sig).astype(bf16))
    fold(jnp.concatenate(done, axis=1), outs)


def rows_kernel(outs, rows_ref, *refs):
    matrices = [rows_ref[i] for i in range(1 + FOLD)]
    rows = from_slots(matrices, refs[:-outs]).astype(bf16)
    width = rows.shape[1] // outs
    for i, ref in enumerate(refs[-outs:]):
        ref[...] = rows[:, i * width : (i + 1) * width]


def head_cols(head):
    return slice(head * HD, (head + 1) * HD)


ACROSS = [(0, 1), (1, 0), (2, 3), (3, 2)]


def by_corner(blocks):
    return lax.axis_size("seq") == 4 and blocks == 3


def shifted_pairs(value, key, blocks):
    if not by_corner(blocks):
        return [[one] + [shifted(one, d) for d in range(1, blocks)] for one in (value, key)]
    key_far = shifted(key, 2)
    value_near = shifted(value, 1)
    value_far = shifted(value, 2)
    key_near = lax.ppermute(key, "seq", ACROSS)
    handed = lax.ppermute(key_far, "seq", ACROSS)
    return [value, value_near, value_far], [key, key_near, key_far, handed]


def shifted_queries(query, blocks):
    if not by_corner(blocks):
        return [shifted(query, -d) for d in range(1, blocks)]
    far = shifted(query, -2)
    near = lax.ppermute(query, "seq", ACROSS)
    return [near, far, lax.ppermute(far, "seq", ACROSS)]


def stack(refs, cols, blocks, corner=0):
    parts = [ref[:, cols] for ref in refs[:blocks]]
    if len(refs) > blocks:
        at = 0 if corner == 1 else 1
        parts[at] = jnp.where(lax.axis_index("seq") == corner, refs[blocks][:, cols], parts[at])
    return jnp.concatenate(parts, axis=0)


def forward_kernel(blocks, see_ref, gate_in_ref, query_ref, cotan_ref, *refs):
    grad_ref, normed_ref = refs[-2:]
    values, keys = refs[:blocks], refs[blocks:-2]
    scale = HD ** (-0.5)
    see = see_ref[...]
    done = []
    for head in range(HEADS):
        cols = head_cols(head)
        score = dot_nt(query_ref[:, cols], stack(keys, cols, blocks, 2)) * scale
        weight = (score * sigmoid(score) * see).astype(bf16)
        done.append(dot(weight, stack(values, cols, blocks)))
    mixed = jnp.concatenate(done, axis=1)
    row_scale = lax.rsqrt(jnp.mean(mixed * mixed, axis=1, keepdims=True) + eps)
    normed = mixed * row_scale
    grad_norm = cotan_ref[...].astype(f32) * gate_in_ref[...].astype(f32)
    mean = row_scale * jnp.mean(grad_norm * mixed, axis=1, keepdims=True)
    grad_ref[...] = (row_scale * (grad_norm - normed * mean)).astype(bf16)
    normed_ref[...] = normed


def output_kernel(gate_ref, normed_ref, out_ref):
    out_ref[...] = (gate_ref[...].astype(f32) * normed_ref[...]).astype(bf16)


def slope_of(score):
    sig = sigmoid(score)
    return sig, sig * (1.0 + score * (1.0 - sig))


def wires_out(count, refs):
    return [refs[i : i + count] for i in range(0, len(refs), count)]


def query_kernel(
    count, total, blocks, see_ref, query_ref, grad_ref, cotan_ref, normed_ref, slots_ref, *refs
):
    wires = wires_out(count, refs[-total:])
    values, keys = refs[:blocks], refs[blocks:-total]
    scale = HD ** (-0.5)
    see = see_ref[...]
    done = []
    for head in range(HEADS):
        cols = head_cols(head)
        key = stack(keys, cols, blocks, 2)
        _, slope = slope_of(dot_nt(query_ref[:, cols], key) * scale)
        att = dot_nt(grad_ref[:, cols], stack(values, cols, blocks))
        done.append((dot((att * slope * see).astype(bf16), key) * scale).astype(bf16))
    grad_gate = (cotan_ref[...].astype(f32) * normed_ref[...]).astype(bf16)
    parts_to_slots(slots_ref, [grad_gate, jnp.concatenate(done, axis=1)], wires)


def joined(parts, axis):
    return parts[0] if len(parts) == 1 else jnp.concatenate(parts, axis=axis)


def score_kernel(blocks, seen_ref, value_ref, key_ref, query_ref, grad_ref, *refs):
    far = blocks - 2
    queries, (value_sum_ref, key_sum_ref), kept = refs[:far], refs[far : far + 2], refs[far + 2 :]
    rows = key_ref.shape[0]
    scale = HD ** (-0.5)
    seen = joined([seen_ref[:, :rows]] + [seen_ref[:, 2 * rows :]] * (far > 0), 1)
    for head in range(HEADS):
        cols = head_cols(head)
        own, grad = query_ref[:, cols], grad_ref[:, cols]
        query = joined([own] + [ref[:, cols] for ref in queries], 0)
        score = dot_nt(key_ref[:, cols], query) * scale
        sig, slope = slope_of(score)
        weight = (score * sig * seen).astype(bf16)
        slope = slope * seen
        att = dot_nt(value_ref[:, cols], grad)
        value_sum_ref[:, cols] = dot(weight[:, :rows], grad)
        key_sum_ref[:, cols] = dot((att * slope[:, :rows]).astype(bf16), own)
        for ref, one in zip(kept, (weight, slope)):
            ref[head] = one[:, rows:]


def key_kernel(count, total, blocks, seen_ref, value_ref, key_ref, slots_ref, *refs):
    later, far = blocks - 1, blocks - 2
    value_sum_ref, key_sum_ref = refs[:2]
    kept, refs = refs[2 : 2 + 2 * (far > 0)], refs[2 + 2 * (far > 0) :]
    grads, queries = refs[:later], refs[later:-total]
    wires = wires_out(count, refs[-total:])
    rows = key_ref.shape[0]
    scale = HD ** (-0.5)
    seen = seen_ref[:, rows : 2 * rows]
    values, keys = [], []
    for head in range(HEADS):
        cols = head_cols(head)
        query = stack(queries, cols, later, 1)
        score = dot_nt(key_ref[:, cols], query[:rows]) * scale
        sig, slope = slope_of(score)
        near = ((score * sig * seen).astype(bf16), slope * seen)
        weight, slope = [joined([one] + [ref[head] for ref in kept[i : i + 1]], 1) for i, one in enumerate(near)]
        grad = stack(grads, cols, later)
        grad_score = (dot_nt(value_ref[:, cols], grad) * slope).astype(bf16)
        value = dot(weight, grad) + value_sum_ref[:, cols]
        key = dot(grad_score, query) + key_sum_ref[:, cols]
        values.append(value.astype(bf16))
        keys.append((key * scale).astype(bf16))
    parts = [jnp.concatenate(one, axis=1) for one in (values, keys)]
    parts_to_slots(slots_ref, parts, wires)


def owner_term(parts, refs, slope_ref, w_ref):
    width = HEADS * HD
    grad_pre = (unfold(refs).astype(f32) * slope_ref[...]).astype(bf16)
    term = None
    for i, part in enumerate(parts):
        one = dot_nt(
            grad_pre[:, i * width : (i + 1) * width], w_ref[:, part * width : (part + 1) * width]
        )
        term = one if term is None else term + one
    return term


def term_kernel(parts, slope_ref, w_ref, *refs):
    refs[-1][...] = owner_term(parts, refs[:-1], slope_ref, w_ref)


def last_term_kernel(count, parts, slope_ref, w_ref, *refs):
    ins, others, outs = refs[:count], refs[count:-count], refs[-count:]
    term = owner_term(parts, ins, slope_ref, w_ref)
    for other_ref in others:
        term = term + other_ref[...]
    fold(term.astype(bf16), outs)


def leave_kernel(count, rows_ref, events_ref, gain_ref, *refs):
    matrices = [rows_ref[i] for i in range(1 + FOLD)]
    wires = wires_out(count, refs[:-1])
    scaled = sum(from_slots(matrices, wire) for wire in wires) * gain_of(gain_ref)
    events = events_ref[...].astype(f32)
    row_inv = lax.rsqrt(jnp.mean(events * events, axis=1, keepdims=True) + eps)
    normed = events * row_inv
    mean = jnp.mean(scaled * normed, axis=1, keepdims=True)
    refs[-1][...] = (row_inv * (scaled - normed * mean)).astype(bf16)


def exchange(blocks):
    done = exchanged(blocks)
    if 1 < len(blocks) < lax.axis_size("user"):
        others = jnp.concatenate([block[MAIN:] for block in done], axis=0)
        done += [lax.ppermute(others, "user", [(i, i ^ 1) for i in range(lax.axis_size("user"))])]
    return done


def exchanged(blocks):
    count = lax.axis_size("user")
    if len(blocks) == 1:
        wire = blocks[0].reshape(-1, MAIN, blocks[0].shape[1])
        done = lax.all_to_all(wire, "user", split_axis=0, concat_axis=0, tiled=True)
        return [done.reshape(blocks[0].shape)]
    done = list(blocks)
    merged = count // len(blocks)
    for k in range(1, len(blocks)):
        done[k] = lax.ppermute(blocks[k], "user", [(i, i ^ (merged * k)) for i in range(count)])
    return done


def shifted(block, distance):
    count = lax.axis_size("seq")
    route = [((i - distance) % count, i) for i in range(count)]
    return lax.ppermute(block, "seq", route)


def wires_of(boxes):
    cols = boxes[0].shape[1]
    return [jnp.stack([box.reshape(SCEN, MAIN, cols) for box in boxes], axis=1).reshape(-1, cols)]


def slices_of(split, box):
    cols = box.shape[1]
    blocks = box.reshape(SCEN, split, MAIN, cols)
    return [blocks[:, i].reshape(-1, cols) for i in range(split)]


def shards(events, scenario, lengths, offsets, gain, w_proj, cotangent):
    n_seq = lax.axis_size("seq")
    n_user = lax.axis_size("user")
    split = n_user // SCEN
    rows, feats = events.shape[1:]
    width = HEADS * HD
    longest = n_seq * rows // 2
    reach = min(REACH, n_seq - 1, (longest - 2) // rows + 1)
    blocks = reach + 1
    direct = split == 1
    senders = SCEN if direct else 1

    def wire(rows, cols, merged=1):
        count = rows // (MAIN * merged) if direct else 1
        return [shape((rows // count, cols * (FOLD + 1) // FOLD), bf16)] * count

    slots = wire(SCEN * MAIN, feats)
    matrices = shape((1 + FOLD, rows, SCEN * MAIN), bf16)
    events, w_local, cotan = events[0], w_proj[0], cotangent[0]
    gain = gain.reshape(-1, LANES)

    to_slot, *outbox = call(
        functools.partial(enter_kernel, direct),
        [matrices] + slots,
        [events, gain, scenario],
        [pltpu.HBM] * 3,
        [
            pltpu.VMEM(events.shape, bf16),
            pltpu.VMEM(gain.shape, f32),
            pltpu.VMEM(scenario.shape, jnp.int32),
            pltpu.SemaphoreType.DMA((3,)),
        ],
    )
    inbound = exchange(outbox if direct else wires_of(outbox * split))
    small = jnp.concatenate([lengths, offsets, scenario], axis=1)
    w_local, to_row, see, seen = call(
        functools.partial(mask_kernel, direct, blocks, lengths.shape[1]),
        [shape(w_local.shape, bf16), matrices] + [shape((rows, blocks * rows), f32)] * 2,
        [w_local, small],
        [pltpu.HBM],
        [pltpu.SemaphoreType.DMA((4,))],
    )

    def project(parts, early=False, sums=()):
        cols = len(parts) * width
        box = wire(n_user * MAIN, cols)
        *done, slope = call(
            functools.partial(project_kernel, senders, parts, early, len(sums) > 0),
            box + [shape((n_user * CAP, cols), f32)] * (1 + len(sums)),
            [w_local] + inbound + list(sums),
        )
        return exchange(done[: len(box)]), slope, *done[len(box) :]

    def rows_of(box, parts=2):
        outs = [shape((rows, width), bf16)] * parts
        return call(functools.partial(rows_kernel, parts), outs, [to_row] + box)

    if direct:
        pair_parts, query_parts = (1, 3), (0, 2)
        pair_back, pair_sums = project(pair_parts, early=True)
        query_back, query_slope, pair_slope = project(query_parts, sums=[pair_sums])
        value, key = rows_of(pair_back)
        gate, query = rows_of(query_back)
    else:
        (box,), slope = project((0,))[:2]
        gate, value, query, key = [rows_of([part], 1)[0] for part in slices_of(split, box)]
    values, keys = shifted_pairs(value, key, blocks)
    queries = shifted_queries(query, blocks)
    half = shape((rows, width), bf16)
    grad_own, normed = call(
        functools.partial(forward_kernel, blocks),
        [half, shape((rows, width), f32)],
        [see, gate, query, cotan] + values + keys,
    )
    grads = [shifted(grad_own, -d) for d in range(1, blocks)]

    def boxes(merged=1):
        cols = 2 * width if direct else width
        return wire(SCEN * MAIN, cols, merged) * (1 if direct else 2)

    query_grad = call(
        functools.partial(query_kernel, len(boxes(2)) if direct else 1, len(boxes(2)), blocks),
        boxes(2),
        [see, query, grad_own, cotan, normed, to_slot] + values + keys,
    )
    far = reach - 1
    each = (HEADS, rows, far * rows)
    scores = call(
        functools.partial(score_kernel, blocks),
        [shape((rows, width), f32)] * 2 + [shape(each, bf16), shape(each, f32)] * (far > 0),
        [seen, value, key, query, grad_own] + queries[1:reach],
    )
    pair_grad = call(
        functools.partial(key_kernel, senders, len(boxes()), blocks),
        boxes(),
        [seen, value, key, to_slot, *scores] + grads + queries,
    )
    term = shape((n_user * CAP, feats), f32)
    if direct:
        (query_term,) = call(
            functools.partial(term_kernel, query_parts),
            [term],
            [query_slope, w_local] + exchange(query_grad),
        )
        last_parts, last = pair_parts, [pair_slope, w_local] + exchange(pair_grad) + [query_term]
    else:
        order = [query_grad[0], pair_grad[0], query_grad[1], pair_grad[1]]
        last_parts, last = (0,), [slope, w_local] + exchange(wires_of(order))
    term_box = call(
        functools.partial(last_term_kernel, senders, last_parts), wire(n_user * MAIN, feats), last
    )
    (output,) = call(output_kernel, [half], [gate, normed])
    term_back = exchange(term_box)
    (grad_events,) = call(
        functools.partial(leave_kernel, senders),
        [shape((rows, feats), bf16)],
        [to_row, events, gain] + (term_back if direct else slices_of(split, term_back[0])),
    )
    return output[None], grad_events[None]


def solution(mesh):
    placed = (
        P("user", "seq", None),
        P("user", "seq"),
        P("user", None),
        P("user", None),
        P(),
        P("user", None, None),
        P("user", "seq", None),
    )
    return jax.shard_map(
        shards,
        mesh=mesh,
        in_specs=placed,
        out_specs=(P("user", "seq", None), P("user", "seq", None)),
        check_vma=False,
    )
```

```python
import functools

import jax
import jax.numpy as jnp
from jax import lax
from jax.experimental import pallas as pl
from jax.experimental.pallas import tpu as pltpu
from jax.sharding import PartitionSpec as P


HEADS = 6
HD = 128
SCEN = 8
MB = 128
CAP = 20
REACH = 4

MAIN = 16
EXTRA = CAP - MAIN
FOLD = MAIN // EXTRA

VMEM_LIMIT = 24 << 20
LANES = 128

eps = 1e-05
f32 = jnp.float32
bf16 = jnp.bfloat16
NT = (((1,), (1,)), ((), ()))


def call(kernel, outs, operands, spaces=(), scratch=(), flops=1 << 24, limit=VMEM_LIMIT):
    spaces = list(spaces) + [pltpu.VMEM] * (len(operands) - len(spaces))
    moved = sum(o.size * o.dtype.itemsize for o in list(outs) + list(operands))
    operands = [
        pltpu.with_memory_space_constraint(operand, space) if space == pltpu.HBM else operand
        for operand, space in zip(operands, spaces)
    ]
    return pl.pallas_call(
        kernel,
        out_shape=tuple(outs),
        in_specs=[pl.BlockSpec(memory_space=space) for space in spaces],
        out_specs=tuple(pl.BlockSpec(memory_space=pltpu.VMEM) for _ in outs),
        scratch_shapes=list(scratch),
        cost_estimate=pl.CostEstimate(flops=flops, bytes_accessed=moved, transcendentals=0),
        compiler_params=pltpu.CompilerParams(vmem_limit_bytes=limit),
    )(*operands)


def shape(dims, dtype):
    return jax.ShapeDtypeStruct(dims, dtype)


def dot(a, b):
    return jnp.dot(a, b, preferred_element_type=f32)


def dot_nt(a, b):
    return lax.dot_general(a, b, NT, preferred_element_type=f32)


def sigmoid(v):
    return 0.5 * jnp.tanh(0.5 * v) + 0.5


def iotas(rows, cols):
    return (
        lax.broadcasted_iota(jnp.int32, (rows, cols), 0),
        lax.broadcasted_iota(jnp.int32, (rows, cols), 1),
    )


def hot(condition):
    return jnp.where(condition, 1.0, 0.0).astype(bf16)


def load(refs, cols):
    if swapped(refs):
        parts = []
        for i, ref in enumerate(refs[:-1]):
            parts += [ref[:MAIN, cols], refs[-1][i * MAIN : (i + 1) * MAIN, cols]]
    else:
        parts = [ref[:, cols] for ref in refs]
    return parts[0] if len(parts) == 1 else jnp.concatenate(parts, axis=0)


def swapped(refs):
    return len(refs) > 1 and refs[0].shape[0] == 2 * MAIN


def rows_in(refs):
    return 2 * refs[-1].shape[0] if swapped(refs) else sum(ref.shape[0] for ref in refs)


def store(refs, cols, value):
    rows = refs[0].shape[0]
    for i, ref in enumerate(refs):
        ref[:, cols] = value[i * rows : (i + 1) * rows]


def main_cols(refs):
    return refs[0].shape[1] * FOLD // (FOLD + 1)


def slot_matrices(scen_row, by_slot):
    rows = scen_row.shape[1]
    down, along = iotas(rows, rows)
    scen_b = jnp.broadcast_to(scen_row.astype(f32), (rows, rows))
    scen_col = jnp.sum(jnp.where(down == along, scen_b, 0.0), axis=1, keepdims=True)
    same = scen_b == scen_col
    if by_slot:
        scen = scen_row.astype(f32)
        rank = jnp.sum(jnp.where(same & (down < along), 1.0, 0.0), axis=0, keepdims=True)
        down, along = iotas(SCEN * MAIN, rows)
        slot = down.astype(f32)
    else:
        scen = scen_col
        rank = jnp.sum(jnp.where(same & (along < down), 1.0, 0.0), axis=1, keepdims=True)
        down, along = iotas(rows, SCEN * MAIN)
        slot = along.astype(f32)
    main = jnp.where(rank < MAIN, scen * MAIN + rank, -1.0)
    out = [hot(slot == main)]
    for piece in range(FOLD):
        extra = jnp.where(rank >= MAIN, scen * MAIN + EXTRA * piece + (rank - MAIN), -1.0)
        out.append(hot(slot == extra))
    return out


def to_slots(matrices, value, refs):
    cols = value.shape[1]
    piece = cols // FOLD
    store(refs, slice(0, cols), dot(matrices[0], value).astype(bf16))
    extra = dot(matrices[1], value[:, :piece])
    for part in range(1, FOLD):
        extra = extra + dot(matrices[1 + part], value[:, part * piece : (part + 1) * piece])
    store(refs, slice(cols, cols + piece), extra.astype(bf16))


def from_slots(matrices, refs):
    cols = main_cols(refs)
    piece = cols // FOLD
    extra = load(refs, slice(cols, cols + piece))
    out = []
    for part in range(FOLD):
        left = jnp.concatenate([matrices[0], matrices[1 + part]], axis=1)
        right = jnp.concatenate([load(refs, slice(part * piece, (part + 1) * piece)), extra], axis=0)
        out.append(dot(left, right))
    return jnp.concatenate(out, axis=1)


def parts_to_slots(slots_ref, parts, wires):
    matrices = [slots_ref[i] for i in range(1 + FOLD)]
    if len(wires) == 1:
        parts = [jnp.concatenate(parts, axis=1)]
    for part, refs in zip(parts, wires):
        to_slots(matrices, part, refs)


def extra_matrix(count, part, by_row):
    if by_row:
        down, along = iotas(count * EXTRA, count * MAIN)
    else:
        along, down = iotas(count * MAIN, count * EXTRA)
    group = sum((down >= EXTRA * i).astype(jnp.int32) for i in range(1, count))
    return hot(along == down + group * (MAIN - EXTRA) + EXTRA * part)


def unfold(refs):
    count = rows_in(refs) // MAIN
    cols = main_cols(refs)
    extra = load(refs, slice(cols, cols + cols // FOLD))
    pieces = [dot(extra_matrix(count, part, True), extra) for part in range(FOLD)]
    extra = jnp.concatenate(pieces, axis=1).astype(bf16)
    return jnp.concatenate([load(refs, slice(0, cols)), extra], axis=0)


def fold(value, refs):
    rows, cols = sum(ref.shape[0] for ref in refs), value.shape[1]
    count = rows // MAIN
    piece = cols // FOLD
    store(refs, slice(0, cols), value[:rows])
    extra = sum(
        dot(extra_matrix(count, part, False), value[rows:, part * piece : (part + 1) * piece])
        for part in range(FOLD)
    )
    store(refs, slice(cols, cols + piece), extra.astype(bf16))


def own_scenarios(scen_ref, direct):
    return scen_ref[...] ^ lax.axis_index("user") if direct else scen_ref[...]


def gain_of(gain_ref):
    return jnp.concatenate([gain_ref[i : i + 1] for i in range(gain_ref.shape[0])], axis=1)


def enter_kernel(direct, events_hbm, gain_hbm, scen_hbm, slots_ref, *refs):
    events_ref, gain_ref, scen_ref, sems = refs[-4:]
    refs = refs[:-4]
    loads = [
        pltpu.make_async_copy(source, target, sems.at[i])
        for i, (source, target) in enumerate(
            [(events_hbm, events_ref), (gain_hbm, gain_ref), (scen_hbm, scen_ref)]
        )
    ]
    for load_ in reversed(loads):
        load_.start()
    loads[2].wait()
    matrices = slot_matrices(own_scenarios(scen_ref, direct), True)
    for i, matrix in enumerate(matrices):
        slots_ref[i] = matrix
    loads[1].wait()
    loads[0].wait()
    events = events_ref[...].astype(f32)
    row_inv = lax.rsqrt(jnp.mean(events * events, axis=1, keepdims=True) + eps)
    normed = (events * row_inv * gain_of(gain_ref)).astype(bf16)
    to_slots(matrices, normed, refs)


def history_of(pos, ends):
    return sum((pos >= end).astype(jnp.int32) for end in ends)


def limit_of(history, limits):
    return sum(jnp.where(history == i, limit, 0) for i, limit in enumerate(limits))


def mask_kernel(
    direct, blocks, histories, w_hbm, small_ref, w_ref, rows_ref, see_ref, seen_ref, sems
):
    count = sems.shape[0]
    depth = w_ref.shape[0] // count
    loads = [
        pltpu.make_async_copy(
            w_hbm.at[pl.ds(i * depth, depth)], w_ref.at[pl.ds(i * depth, depth)], sems.at[i]
        )
        for i in range(count)
    ]
    for load_ in loads:
        load_.start()
    for i, matrix in enumerate(
        slot_matrices(own_scenarios(small_ref.at[:, 2 * histories :], direct), False)
    ):
        rows_ref[i] = matrix
    rows = see_ref.shape[0]
    ends, total = [], 0
    for i in range(histories):
        total = total + small_ref[:, i : i + 1]
        ends.append(total)
    limits = [small_ref[:, i : i + 1] for i in range(histories, 2 * histories)]
    first = lax.axis_index("seq") * rows
    shift = MB.bit_length() - 1

    def visible(query, key):
        query_hist, key_hist = history_of(query, ends), history_of(key, ends)
        near = (query >> shift) - (key >> shift) <= limit_of(query_hist, limits)
        return jnp.where((query_hist == key_hist) & (key <= query) & (key >= 0) & near, 1.0, 0.0)

    down = lax.broadcasted_iota(jnp.int32, (rows, rows), 0)
    along = lax.broadcasted_iota(jnp.int32, (rows, rows), 1)
    for block in range(blocks):
        span = slice(block * rows, (block + 1) * rows)
        see_ref[:, span] = visible(first + down, first - block * rows + along)
        seen_ref[:, span] = visible(first + block * rows + along, first + down)
    for load_ in loads:
        load_.wait()


def project_kernel(count, parts, early, late, w_ref, *refs):
    ins, rest, kept_ref = refs[:count], refs[count:-1], refs[-1]
    if late:
        _, rest[-1][...] = slope_of(rest[0][...])
        rest = rest[1:-1]
    outs = rest
    rows = unfold(ins)
    width = HEADS * HD
    done = []
    for i, part in enumerate(parts):
        pre = dot(rows, w_ref[:, part * width : (part + 1) * width])
        sig = sigmoid(pre)
        cols = slice(i * width, (i + 1) * width)
        kept_ref[:, cols] = pre if early else sig * (1.0 + pre * (1.0 - sig))
        done.append((pre * sig).astype(bf16))
    fold(jnp.concatenate(done, axis=1), outs)


def rows_kernel(outs, rows_ref, *refs):
    matrices = [rows_ref[i] for i in range(1 + FOLD)]
    rows = from_slots(matrices, refs[:-outs]).astype(bf16)
    width = rows.shape[1] // outs
    for i, ref in enumerate(refs[-outs:]):
        ref[...] = rows[:, i * width : (i + 1) * width]


def head_cols(head):
    return slice(head * HD, (head + 1) * HD)


ACROSS = [(0, 1), (1, 0), (2, 3), (3, 2)]


def by_corner(blocks):
    return lax.axis_size("seq") == 4 and blocks == 3


def shifted_pairs(value, key, blocks):
    if not by_corner(blocks):
        return [[one] + [shifted(one, d) for d in range(1, blocks)] for one in (value, key)]
    key_far = shifted(key, 2)
    value_near = shifted(value, 1)
    value_far = shifted(value, 2)
    key_near = lax.ppermute(key, "seq", ACROSS)
    handed = lax.ppermute(key_far, "seq", ACROSS)
    return [value, value_near, value_far], [key, key_near, key_far, handed]


def shifted_queries(query, blocks):
    if not by_corner(blocks):
        return [shifted(query, -d) for d in range(1, blocks)]
    far = shifted(query, -2)
    near = lax.ppermute(query, "seq", ACROSS)
    return [near, far, lax.ppermute(far, "seq", ACROSS)]


def stack(refs, cols, blocks, corner=0):
    parts = [ref[:, cols] for ref in refs[:blocks]]
    if len(refs) > blocks:
        at = 0 if corner == 1 else 1
        parts[at] = jnp.where(lax.axis_index("seq") == corner, refs[blocks][:, cols], parts[at])
    return jnp.concatenate(parts, axis=0)


def forward_kernel(blocks, see_ref, gate_in_ref, query_ref, cotan_ref, *refs):
    grad_ref, normed_ref = refs[-2:]
    values, keys = refs[:blocks], refs[blocks:-2]
    scale = HD ** (-0.5)
    see = see_ref[...]
    done = []
    for head in range(HEADS):
        cols = head_cols(head)
        score = dot_nt(query_ref[:, cols], stack(keys, cols, blocks, 2)) * scale
        weight = (score * sigmoid(score) * see).astype(bf16)
        done.append(dot(weight, stack(values, cols, blocks)))
    mixed = jnp.concatenate(done, axis=1)
    row_scale = lax.rsqrt(jnp.mean(mixed * mixed, axis=1, keepdims=True) + eps)
    normed = mixed * row_scale
    grad_norm = cotan_ref[...].astype(f32) * gate_in_ref[...].astype(f32)
    mean = row_scale * jnp.mean(grad_norm * mixed, axis=1, keepdims=True)
    grad_ref[...] = (row_scale * (grad_norm - normed * mean)).astype(bf16)
    normed_ref[...] = normed


def output_kernel(gate_ref, normed_ref, out_ref):
    out_ref[...] = (gate_ref[...].astype(f32) * normed_ref[...]).astype(bf16)


def slope_of(score):
    sig = sigmoid(score)
    return sig, sig * (1.0 + score * (1.0 - sig))


def wires_out(count, refs):
    return [refs[i : i + count] for i in range(0, len(refs), count)]


def query_kernel(
    count, total, blocks, see_ref, query_ref, grad_ref, cotan_ref, normed_ref, slots_ref, *refs
):
    wires = wires_out(count, refs[-total:])
    values, keys = refs[:blocks], refs[blocks:-total]
    scale = HD ** (-0.5)
    see = see_ref[...]
    done = []
    for head in range(HEADS):
        cols = head_cols(head)
        key = stack(keys, cols, blocks, 2)
        _, slope = slope_of(dot_nt(query_ref[:, cols], key) * scale)
        att = dot_nt(grad_ref[:, cols], stack(values, cols, blocks))
        done.append((dot((att * slope * see).astype(bf16), key) * scale).astype(bf16))
    grad_gate = (cotan_ref[...].astype(f32) * normed_ref[...]).astype(bf16)
    parts_to_slots(slots_ref, [grad_gate, jnp.concatenate(done, axis=1)], wires)


def joined(parts, axis):
    return parts[0] if len(parts) == 1 else jnp.concatenate(parts, axis=axis)


def score_kernel(blocks, seen_ref, value_ref, key_ref, query_ref, grad_ref, *refs):
    far = blocks - 2
    queries, (value_sum_ref, key_sum_ref), kept = refs[:far], refs[far : far + 2], refs[far + 2 :]
    rows = key_ref.shape[0]
    scale = HD ** (-0.5)
    seen = joined([seen_ref[:, :rows]] + [seen_ref[:, 2 * rows :]] * (far > 0), 1)
    for head in range(HEADS):
        cols = head_cols(head)
        own, grad = query_ref[:, cols], grad_ref[:, cols]
        query = joined([own] + [ref[:, cols] for ref in queries], 0)
        score = dot_nt(key_ref[:, cols], query) * scale
        sig, slope = slope_of(score)
        weight = (score * sig * seen).astype(bf16)
        slope = slope * seen
        att = dot_nt(value_ref[:, cols], grad)
        value_sum_ref[:, cols] = dot(weight[:, :rows], grad)
        key_sum_ref[:, cols] = dot((att * slope[:, :rows]).astype(bf16), own)
        for ref, one in zip(kept, (weight, slope)):
            ref[head] = one[:, rows:]


def key_kernel(count, total, blocks, seen_ref, value_ref, key_ref, slots_ref, *refs):
    later, far = blocks - 1, blocks - 2
    value_sum_ref, key_sum_ref = refs[:2]
    kept, refs = refs[2 : 2 + 2 * (far > 0)], refs[2 + 2 * (far > 0) :]
    grads, queries = refs[:later], refs[later:-total]
    wires = wires_out(count, refs[-total:])
    rows = key_ref.shape[0]
    scale = HD ** (-0.5)
    seen = seen_ref[:, rows : 2 * rows]
    values, keys = [], []
    for head in range(HEADS):
        cols = head_cols(head)
        query = stack(queries, cols, later, 1)
        score = dot_nt(key_ref[:, cols], query[:rows]) * scale
        sig, slope = slope_of(score)
        near = ((score * sig * seen).astype(bf16), slope * seen)
        weight, slope = [joined([one] + [ref[head] for ref in kept[i : i + 1]], 1) for i, one in enumerate(near)]
        grad = stack(grads, cols, later)
        grad_score = (dot_nt(value_ref[:, cols], grad) * slope).astype(bf16)
        value = dot(weight, grad) + value_sum_ref[:, cols]
        key = dot(grad_score, query) + key_sum_ref[:, cols]
        values.append(value.astype(bf16))
        keys.append((key * scale).astype(bf16))
    parts = [jnp.concatenate(one, axis=1) for one in (values, keys)]
    parts_to_slots(slots_ref, parts, wires)


def owner_term(parts, refs, slope_ref, w_ref):
    width = HEADS * HD
    grad_pre = (unfold(refs).astype(f32) * slope_ref[...]).astype(bf16)
    term = None
    for i, part in enumerate(parts):
        one = dot_nt(
            grad_pre[:, i * width : (i + 1) * width], w_ref[:, part * width : (part + 1) * width]
        )
        term = one if term is None else term + one
    return term


def turn_kernel(parts, w_ref, out_ref):
    width, piece = HEADS * HD, 2 * LANES
    for i, part in enumerate(parts):
        for at in range(0, width, piece):
            cols = w_ref[:, part * width + at : part * width + at + piece]
            out_ref[i * width + at : i * width + at + piece] = cols.T


def term_kernel(parts, slope_ref, w_ref, *refs):
    refs[-1][...] = owner_term(parts, refs[:-1], slope_ref, w_ref)


def last_term_kernel(count, parts, turned, slope_ref, w_ref, *refs):
    ins, others, outs = refs[:count], refs[count:-count], refs[-count:]
    if turned:
        term = dot((unfold(ins).astype(f32) * slope_ref[...]).astype(bf16), w_ref[...])
    else:
        term = owner_term(parts, ins, slope_ref, w_ref)
    for other_ref in others:
        term = term + other_ref[...]
    fold(term.astype(bf16), outs)


def leave_kernel(count, rows_ref, events_ref, gain_ref, *refs):
    matrices = [rows_ref[i] for i in range(1 + FOLD)]
    wires = wires_out(count, refs[:-1])
    scaled = sum(from_slots(matrices, wire) for wire in wires) * gain_of(gain_ref)
    events = events_ref[...].astype(f32)
    row_inv = lax.rsqrt(jnp.mean(events * events, axis=1, keepdims=True) + eps)
    normed = events * row_inv
    mean = jnp.mean(scaled * normed, axis=1, keepdims=True)
    refs[-1][...] = (row_inv * (scaled - normed * mean)).astype(bf16)


def exchange(blocks):
    done = exchanged(blocks)
    if 1 < len(blocks) < lax.axis_size("user"):
        others = jnp.concatenate([block[MAIN:] for block in done], axis=0)
        done += [lax.ppermute(others, "user", [(i, i ^ 1) for i in range(lax.axis_size("user"))])]
    return done


def exchanged(blocks):
    count = lax.axis_size("user")
    if len(blocks) == 1:
        wire = blocks[0].reshape(-1, MAIN, blocks[0].shape[1])
        done = lax.all_to_all(wire, "user", split_axis=0, concat_axis=0, tiled=True)
        return [done.reshape(blocks[0].shape)]
    done = list(blocks)
    merged = count // len(blocks)
    for k in range(1, len(blocks)):
        done[k] = lax.ppermute(blocks[k], "user", [(i, i ^ (merged * k)) for i in range(count)])
    return done


def shifted(block, distance):
    count = lax.axis_size("seq")
    route = [((i - distance) % count, i) for i in range(count)]
    return lax.ppermute(block, "seq", route)


def wires_of(boxes):
    cols = boxes[0].shape[1]
    return [jnp.stack([box.reshape(SCEN, MAIN, cols) for box in boxes], axis=1).reshape(-1, cols)]


def slices_of(split, box):
    cols = box.shape[1]
    blocks = box.reshape(SCEN, split, MAIN, cols)
    return [blocks[:, i].reshape(-1, cols) for i in range(split)]


def shards(events, scenario, lengths, offsets, gain, w_proj, cotangent):
    n_seq = lax.axis_size("seq")
    n_user = lax.axis_size("user")
    split = n_user // SCEN
    rows, feats = events.shape[1:]
    width = HEADS * HD
    longest = n_seq * rows // 2
    reach = min(REACH, n_seq - 1, (longest - 2) // rows + 1)
    blocks = reach + 1
    direct = split == 1
    senders = SCEN if direct else 1

    def wire(rows, cols, merged=1):
        count = rows // (MAIN * merged) if direct else 1
        return [shape((rows // count, cols * (FOLD + 1) // FOLD), bf16)] * count

    slots = wire(SCEN * MAIN, feats)
    matrices = shape((1 + FOLD, rows, SCEN * MAIN), bf16)
    events, w_local, cotan = events[0], w_proj[0], cotangent[0]
    gain = gain.reshape(-1, LANES)

    to_slot, *outbox = call(
        functools.partial(enter_kernel, direct),
        [matrices] + slots,
        [events, gain, scenario],
        [pltpu.HBM] * 3,
        [
            pltpu.VMEM(events.shape, bf16),
            pltpu.VMEM(gain.shape, f32),
            pltpu.VMEM(scenario.shape, jnp.int32),
            pltpu.SemaphoreType.DMA((3,)),
        ],
    )
    inbound = exchange(outbox if direct else wires_of(outbox * split))
    small = jnp.concatenate([lengths, offsets, scenario], axis=1)
    w_local, to_row, see, seen = call(
        functools.partial(mask_kernel, direct, blocks, lengths.shape[1]),
        [shape(w_local.shape, bf16), matrices] + [shape((rows, blocks * rows), f32)] * 2,
        [w_local, small],
        [pltpu.HBM],
        [pltpu.SemaphoreType.DMA((4,))],
    )

    def project(parts, early=False, sums=()):
        cols = len(parts) * width
        box = wire(n_user * MAIN, cols)
        *done, slope = call(
            functools.partial(project_kernel, senders, parts, early, len(sums) > 0),
            box + [shape((n_user * CAP, cols), f32)] * (1 + len(sums)),
            [w_local] + inbound + list(sums),
        )
        return exchange(done[: len(box)]), slope, *done[len(box) :]

    def rows_of(box, parts=2):
        outs = [shape((rows, width), bf16)] * parts
        return call(functools.partial(rows_kernel, parts), outs, [to_row] + box)

    if direct:
        pair_parts, query_parts = (1, 3), (0, 2)
        pair_back, pair_sums = project(pair_parts, early=True)
        query_back, query_slope, pair_slope = project(query_parts, sums=[pair_sums])
        value, key = rows_of(pair_back)
        gate, query = rows_of(query_back)
    else:
        (box,), slope = project((0,))[:2]
        gate, value, query, key = [rows_of([part], 1)[0] for part in slices_of(split, box)]
    values, keys = shifted_pairs(value, key, blocks)
    queries = shifted_queries(query, blocks)
    half = shape((rows, width), bf16)
    grad_own, normed = call(
        functools.partial(forward_kernel, blocks),
        [half, shape((rows, width), f32)],
        [see, gate, query, cotan] + values + keys,
    )
    grads = [shifted(grad_own, -d) for d in range(1, blocks)]

    def boxes(merged=1):
        cols = 2 * width if direct else width
        return wire(SCEN * MAIN, cols, merged) * (1 if direct else 2)

    query_grad = call(
        functools.partial(query_kernel, len(boxes(2)) if direct else 1, len(boxes(2)), blocks),
        boxes(2),
        [see, query, grad_own, cotan, normed, to_slot] + values + keys,
    )
    far = reach - 1
    each = (HEADS, rows, far * rows)
    scores = call(
        functools.partial(score_kernel, blocks),
        [shape((rows, width), f32)] * 2 + [shape(each, bf16), shape(each, f32)] * (far > 0),
        [seen, value, key, query, grad_own] + queries[1:reach],
    )
    pair_grad = call(
        functools.partial(key_kernel, senders, len(boxes()), blocks),
        boxes(),
        [seen, value, key, to_slot, *scores] + grads + queries,
    )
    term = shape((n_user * CAP, feats), f32)
    if direct:
        (query_term,) = call(
            functools.partial(term_kernel, query_parts),
            [term],
            [query_slope, w_local] + exchange(query_grad),
        )
        turned = shape((len(pair_parts) * width, feats), bf16)
        (w_rows,) = call(functools.partial(turn_kernel, pair_parts), [turned], [w_local])
        last_parts, last = pair_parts, [pair_slope, w_rows] + exchange(pair_grad) + [query_term]
    else:
        order = [query_grad[0], pair_grad[0], query_grad[1], pair_grad[1]]
        last_parts, last = (0,), [slope, w_local] + exchange(wires_of(order))
    term_box = call(
        functools.partial(last_term_kernel, senders, last_parts, direct),
        wire(n_user * MAIN, feats),
        last,
    )
    (output,) = call(output_kernel, [half], [gate, normed])
    term_back = exchange(term_box)
    (grad_events,) = call(
        functools.partial(leave_kernel, senders),
        [shape((rows, feats), bf16)],
        [to_row, events, gain] + (term_back if direct else slices_of(split, term_back[0])),
    )
    return output[None], grad_events[None]


def solution(mesh):
    placed = (
        P("user", "seq", None),
        P("user", "seq"),
        P("user", None),
        P("user", None),
        P(),
        P("user", None, None),
        P("user", "seq", None),
    )
    return jax.shard_map(
        shards,
        mesh=mesh,
        in_specs=placed,
        out_specs=(P("user", "seq", None), P("user", "seq", None)),
        check_vma=False,
    )
```
